32 devices in a mesh: groups: 2 (over x), chan: 16 (over z, y, core).
Axes of the slice: x: 2, y: 2, z: 4, core: 2. Of those that a mesh axis runs over, the one named last changes fastest.
Arguments:
- waveforms: bfloat16 [10240, 15360], P('chan', 'groups'), parts along dimension 1, may hold values from -250 to 250
- basis: bfloat16 [16, 10240, 200], P(None, 'chan'), may hold values from -1 to 1
- bounds: int32 [2, 768], replicated, may hold values from 0 to 5120, as said below
Outputs:
- detection: float32 [15360], P(('groups', 'chan')), parts along dimension 0
- coefficients: float32 [16, 15360], P(None, ('groups', 'chan')), parts along dimension 1
The draws below stay inside these ranges and needn't reach their ends.
There are 2 independent parts, one for each index of `groups`. The reference program is written for one: setup_inputs(seed, part) draws one part's arguments, and reference() takes and returns one part's arrays. A program takes and returns all parts, laid end to end along the dimension named above; an argument that names none is the same for every part. Nothing has to cross between parts.
Inputs may be any that keep to these rules, and one draw needn't show every extreme that they name: bounds[0, 0] is 0 and every bounds[0, f] is below 160; bounds[1, f] grows roughly in proportion to f and is 5120 at the last bin; where bounds[0, f] exceeds bounds[1, f] nothing passes.
All inputs are finite; a program needn't handle non-finite values.
Results may differ from the reference program's by a relative error of at most 0.017.
Values may be sent and summed in bfloat16 or wider, within the bound.
A program may use at most 128 MiB of HBM per device.

```python
import math
import jax
import jax.numpy as jnp
from jax import lax

C = 10240
FRAME_SPAN = 7680
F = 768
R = 16
L = 200


def draw_waveforms(key, part):
    noise_key, scale_key = jax.random.split(key, 2)
    channel_ramp = 1.0 + 2.0 * jnp.arange(C, dtype=jnp.float32) / C
    spread = jnp.exp(jax.random.uniform(scale_key, (C, 1), jnp.float32, 0.0, math.log(10.0)))
    background_clutter = jnp.clip(jax.random.normal(noise_key, (C, FRAME_SPAN), jnp.float32), -5.0, 5.0)
    return (background_clutter * spread * channel_ramp[:, None]).astype(jnp.bfloat16)


def draw_basis(key, part):
    noise_key, scale_key = jax.random.split(jax.random.fold_in(key, 7), 2)
    raw_noise = jnp.clip(jax.random.normal(noise_key, (R, C, L), jnp.float32), -5.0, 5.0)
    mixed_taps = raw_noise + 0.6 * jnp.roll(raw_noise, 1, axis=0)
    channel_ramp = 1.0 + 2.0 * jnp.arange(C, dtype=jnp.float32) / C
    amplitude = jnp.exp(jax.random.uniform(scale_key, (1, C, 1), jnp.float32, 0.0, math.log(4.0)))
    amplitude = amplitude * channel_ramp[None, :, None]
    return (mixed_taps * amplitude / (3.0 * jnp.sqrt(jnp.float32(C * L)))).astype(jnp.bfloat16)


def draw_bounds(key, part):
    low_key, high_key = jax.random.split(jax.random.fold_in(key, 11), 2)
    slot_indices = jnp.arange(F, dtype=jnp.int32)
    half_count = C // 2
    upper_edge = jnp.minimum(half_count, (slot_indices + 1) * half_count // F + jax.random.randint(high_key, (F,), 0, C // 16, dtype=jnp.int32))
    lower_cutoff = jnp.where(slot_indices == 0, 0, jax.random.randint(low_key, (F,), 0, C // 64, dtype=jnp.int32))
    return jnp.stack([lower_cutoff, upper_edge]).astype(jnp.int32)


def setup_inputs(seed: int = 0, part: int = 0) -> dict:
    keys = jax.random.split(jax.random.key(seed), 4)
    part_keys = jax.random.split(jax.random.fold_in(keys[3], part), 4)
    waveforms = draw_waveforms(jax.random.fold_in(jax.random.fold_in(keys[3], part), 71), part)
    basis = draw_basis(jax.random.fold_in(keys[3], 71), part)
    bounds = draw_bounds(jax.random.fold_in(keys[3], 71), part)
    return {"waveforms": waveforms, "basis": basis, "bounds": bounds}


def settle(values):
    return lax.optimization_barrier(values.astype(jnp.bfloat16)).astype(jnp.float32)

def half_spectrum(real_part, imag_part, recorded_readings):
    slot_indices = jnp.arange(real_part.shape[-1], dtype=jnp.int32)
    imag_kept = jnp.where(slot_indices == 0, jnp.zeros_like(imag_part), imag_part)
    combined = real_part + 1j * imag_kept
    filler = jnp.zeros(real_part.shape[:-1] + (recorded_readings // 2 + 1 - real_part.shape[-1],), dtype=combined.dtype)
    return jnp.concatenate([combined, filler], axis=-1)

def reference(waveforms, basis, bounds):
    signal = waveforms.astype(jnp.float32)
    spectrum = jnp.fft.rfft(signal, axis=1)[:, :F]
    spectrum_real = settle(jnp.real(spectrum))
    spectrum_imag = settle(jnp.imag(spectrum))
    wavenumbers = jnp.fft.fft(spectrum_real + 1j * spectrum_imag, axis=0)
    wave_ids = jnp.arange(C, dtype=jnp.int32)
    magnitude = jnp.where(wave_ids > C // 2, C - wave_ids, wave_ids)[:, None]
    passing = (magnitude >= bounds[0][None, :]) & (magnitude <= bounds[1][None, :])
    passed = jnp.where(passing, wavenumbers, jnp.zeros_like(wavenumbers))
    filtered = jnp.fft.ifft(passed, axis=0)
    filtered_real = settle(jnp.real(filtered))
    filtered_imag = settle(jnp.imag(filtered))
    traces = jnp.fft.irfft(half_spectrum(filtered_real, filtered_imag, FRAME_SPAN), n=FRAME_SPAN, axis=1)
    trace_power = lax.optimization_barrier(jnp.sum(traces * traces, axis=0))
    extended = jnp.concatenate([trace_power, trace_power[:L]])
    running = jnp.concatenate([jnp.zeros((1,), extended.dtype), jnp.cumsum(extended)])
    energy = running[L:L + FRAME_SPAN] - running[:FRAME_SPAN]
    filtered_full = filtered_real + 1j * filtered_imag

    def project(subspace_vector):
        transformed = jnp.fft.rfft(subspace_vector.astype(jnp.float32), n=FRAME_SPAN, axis=1)[:, :F]
        product = jnp.conj(transformed) * filtered_full
        return jnp.stack([lax.optimization_barrier(jnp.sum(jnp.real(product), axis=0)), lax.optimization_barrier(jnp.sum(jnp.imag(product), axis=0))])
    spectra = lax.map(project, basis)
    correlation = jnp.fft.irfft(half_spectrum(spectra[:, 0], spectra[:, 1], FRAME_SPAN), n=FRAME_SPAN, axis=1)
    flattened = basis.astype(jnp.float32).reshape(R, C * L)
    gram_matrix = jnp.dot(flattened, flattened.T, precision=lax.Precision.HIGHEST)
    energy_threshold = energy / (C * L) + 1e-06
    solved = jnp.linalg.solve(gram_matrix, correlation)
    detection = lax.optimization_barrier(jnp.sum(correlation * solved, axis=0)) / (R * energy_threshold)
    coefficients = correlation / jnp.sqrt(energy_threshold)[None, :]
    return (detection, coefficients)
```

```python
import functools
import math

import jax
import jax.numpy as jnp
import numpy as np
from jax import lax
from jax.experimental import pallas as pl
from jax.experimental.pallas import tpu as pltpu
from jax.sharding import PartitionSpec as P

radix = 12
half = radix // 2
lanes = 128
highest = lax.Precision.HIGHEST
bf16 = jnp.bfloat16
f32 = jnp.float32
vmem_limit = 60 * 1024 * 1024


def even_parts(x0, x6, s):
    r = math.sqrt(3.0) / 2.0
    s1, s2, s3, s4, s5 = s
    u, v = x0 + x6, x0 - x6
    e24, d24, e15, d15 = s2 + s4, s2 - s4, s1 + s5, s1 - s5
    even0, odd0 = u + e24, e15 + s3
    even1, odd1 = v + 0.5 * d24, r * d15
    even2, odd2 = u - 0.5 * e24, 0.5 * e15 - s3
    return (
        even0 + odd0,
        even1 + odd1,
        even2 + odd2,
        v - d24,
        even2 - odd2,
        even1 - odd1,
        even0 - odd0,
    )


def odd_parts(d):
    r = math.sqrt(3.0) / 2.0
    d1, d2, d3, d4, d5 = d
    e15, m15 = d1 + d5, d1 - d5
    odd1, even1 = 0.5 * e15 + d3, r * (d2 + d4)
    odd2, even2 = r * m15, r * (d2 - d4)
    return (odd1 + even1, odd2 + even2, e15 - d3, odd2 - even2, odd1 - even1)


def bin_order(frequencies):
    ids = np.arange(frequencies)
    groups = [np.concatenate([ids[ids % radix == 0], ids[ids % radix == half]])]
    signs = [np.ones(frequencies // half)]
    for q in range(1, half):
        plus, minus = ids[ids % radix == q], ids[ids % radix == radix - q]
        groups.append(np.concatenate([plus, minus]))
        signs.append(np.concatenate([np.ones(len(plus)), -np.ones(len(minus))]))
    return np.stack(groups), np.stack(signs)


def time_table(frequencies, readings, fold):
    width = readings // radix
    groups, signs = bin_order(frequencies)
    theta = (groups[:, :, None] * np.arange(width)[None, None, :] % readings) * (
        2.0 * np.pi / readings
    )
    cos, sin = np.cos(theta), np.sin(theta)
    sg = signs[:, :, None]
    real = np.concatenate([cos, -sg * sin], axis=2)
    imag = np.concatenate([-sin, -sg * cos], axis=2)
    first = (groups[0] % radix == 0)[:, None]
    real[0] = np.concatenate([np.where(first, cos[0], 0), np.where(first, 0, cos[0])], axis=1)
    imag[0] = np.concatenate([np.where(first, -sin[0], 0), np.where(first, 0, -sin[0])], axis=1)
    count = groups.shape[1]
    both = np.stack([real, imag], axis=1).reshape(half, 2, count // fold, fold, 2 * width)
    return both.transpose(0, 2, 1, 3, 4).reshape(half, 2 * count, 2 * width)


def row_bins(frequencies, fold):
    order = bin_order(frequencies)[0].reshape(-1, 1, fold)
    return np.broadcast_to(order, (order.shape[0], 2, fold)).reshape(-1)


def spectrum_kernel(x_ref, table_ref, out_ref, y_ref):
    rows, readings = x_ref.shape
    width = readings // radix
    for r0 in range(0, rows, 16):
        rs = slice(r0, r0 + 16)
        for b0 in range(0, width, lanes):
            x = [
                x_ref[rs, a * width + b0 : a * width + b0 + lanes].astype(f32)
                for a in range(radix)
            ]
            yr = even_parts(x[0], x[half], [x[a] + x[radix - a] for a in range(1, half)])
            ys = odd_parts([x[a] - x[radix - a] for a in range(1, half)])
            left = slice(b0, b0 + lanes)
            right = slice(width + b0, width + b0 + lanes)
            y_ref[0, rs, left] = yr[0].astype(bf16)
            y_ref[0, rs, right] = yr[half].astype(bf16)
            for q in range(1, half):
                y_ref[q, rs, left] = yr[q].astype(bf16)
                y_ref[q, rs, right] = ys[q - 1].astype(bf16)
    count = table_ref.shape[1]
    for g in range(half):
        out_ref[g * count : (g + 1) * count, :] = lax.dot_general(
            table_ref[g], y_ref[g], (((1,), (1,)), ((), ())), preferred_element_type=f32
        ).astype(bf16)


def time_spectrum(waveforms, table):
    channels, readings = waveforms.shape
    block = lanes if channels % lanes == 0 else channels
    rows = table.shape[0] * table.shape[1]
    return pl.pallas_call(
        spectrum_kernel,
        out_shape=jax.ShapeDtypeStruct((rows, channels), bf16),
        grid=(channels // block,),
        in_specs=[
            pl.BlockSpec((block, readings), lambda i: (i, 0)),
            pl.BlockSpec(table.shape, lambda i: (0, 0, 0)),
        ],
        out_specs=pl.BlockSpec((rows, block), lambda i: (0, i)),
        scratch_shapes=[pltpu.VMEM((half, block, 2 * readings // radix), bf16)],
        compiler_params=pltpu.CompilerParams(vmem_limit_bytes=vmem_limit),
        name="time_spectrum",
    )(waveforms, table)


def power_kernel(f_ref, table_ref, out_ref, z_ref):
    rows = f_ref.shape[1]
    width = z_ref.shape[2] // 2
    count = table_ref.shape[1]

    @pl.when(pl.program_id(0) == 0)
    def _():
        out_ref[...] = jnp.zeros_like(out_ref)

    for g in range(half):
        z_ref[g] = lax.dot_general(
            f_ref[g * count : (g + 1) * count, :],
            table_ref[g],
            (((0,), (0,)), ((), ())),
            preferred_element_type=f32,
        )
    step = 16
    for b0 in range(0, width, lanes):
        left = slice(b0, b0 + lanes)
        right = slice(width + b0, width + b0 + lanes)
        for r0 in range(0, rows, step):
            rs = slice(r0, r0 + step)
            zr = [z_ref[g, rs, left] for g in range(half)]
            zs = [z_ref[g, rs, right] for g in range(half)]
            even = even_parts(zr[0], zs[0], zr[1:])
            odd = odd_parts(zs[1:])
            for a in range(radix):
                m = min(a, radix - a)
                value = even[m]
                if 0 < a < half:
                    value = value + odd[m - 1]
                if a > half:
                    value = value - odd[m - 1]
                square = value * value
                total = square[0:8]
                for s in range(8, step, 8):
                    total = total + square[s : s + 8]
                out_ref[a, :, left] += total


def time_power(filtered, table):
    rows, channels = filtered.shape
    block = lanes if channels % lanes == 0 else channels
    width = table.shape[2] // 2
    pieces = pl.pallas_call(
        power_kernel,
        out_shape=jax.ShapeDtypeStruct((radix, 8, width), f32),
        grid=(channels // block,),
        in_specs=[
            pl.BlockSpec((rows, block), lambda i: (0, i)),
            pl.BlockSpec(table.shape, lambda i: (0, 0, 0)),
        ],
        out_specs=pl.BlockSpec((radix, 8, width), lambda i: (0, 0, 0)),
        scratch_shapes=[pltpu.VMEM((half, block, 2 * width), f32)],
        compiler_params=pltpu.CompilerParams(vmem_limit_bytes=vmem_limit),
        name="time_power",
    )(filtered, table)
    return jnp.sum(pieces, axis=1).reshape(-1)


def filter_tables(full_count, block_count, parts):
    n2 = lanes
    n1 = full_count // n2
    order = np.arange(n1).reshape(block_count, parts).T.reshape(-1)
    k1, k2, j = np.arange(n1), np.arange(n2), np.arange(n2)
    a1 = 2.0 * np.pi * ((k1[:, None] * order[None, :]) % n1) / n1
    a2 = 2.0 * np.pi * ((j[:, None] * k2[None, :]) % n2) / n2
    at = 2.0 * np.pi * ((k1[:, None] * j[None, :]) % full_count) / full_count
    c1, s1, c2, s2 = np.cos(a1), np.sin(a1), np.cos(a2), np.sin(a2)
    first = np.block([[c1, s1], [-s1, c1]])
    second = np.block([[c2, -s2], [s2, c2]])
    twist = np.stack([np.cos(at), np.sin(at)])
    wave = k1[:, None] + n1 * k2[None, :]
    magnitude = np.minimum(wave, full_count - wave).astype(np.int32)
    return (
        jnp.asarray(first, bf16),
        jnp.asarray(second, bf16),
        jnp.asarray(first.T.copy(), bf16),
        jnp.asarray(second.T.copy(), bf16),
        jnp.asarray(twist, f32),
        jnp.asarray(magnitude),
    )


def filter_kernel(fold, edges_ref, scale_ref, x_ref, w1_ref, w2_ref, v1_ref, v2_ref, tw_ref, mag_ref, o_ref):
    step = pl.program_id(0)
    devices = x_ref.shape[0]
    parts = x_ref.shape[2] // lanes
    n1 = mag_ref.shape[0]
    pieces = []
    for ri in range(2):
        for p in range(parts):
            piece = x_ref[:, ri * fold : (ri + 1) * fold, p * lanes : (p + 1) * lanes]
            pieces.append(jnp.swapaxes(piece.astype(f32), 0, 1).astype(bf16))
    stacked = jnp.concatenate(
        [jnp.concatenate([piece[fi] for piece in pieces], axis=0) for fi in range(fold)], axis=1
    )
    waves = jnp.dot(w1_ref[...], stacked, preferred_element_type=f32)
    tc, ts = tw_ref[0], tw_ref[1]
    rows = []
    for fi in range(fold):
        col = slice(fi * lanes, (fi + 1) * lanes)
        re, im = waves[:n1, col], waves[n1:, col]
        rows.append(
            jnp.concatenate([re * tc + im * ts, im * tc - re * ts], axis=1).astype(bf16)
        )
    waves = jnp.dot(jnp.concatenate(rows, axis=0), w2_ref[...], preferred_element_type=f32)
    mag = mag_ref[...]
    rows = []
    for fi in range(fold):
        low, high = edges_ref[0, step * fold + fi], edges_ref[1, step * fold + fi]
        passing = (mag >= low) & (mag <= high)
        block = waves[fi * n1 : (fi + 1) * n1]
        rows.append(
            jnp.concatenate(
                [
                    jnp.where(passing, block[:, :lanes], 0.0),
                    jnp.where(passing, block[:, lanes:], 0.0),
                ],
                axis=1,
            ).astype(bf16)
        )
    waves = jnp.dot(jnp.concatenate(rows, axis=0), v2_ref[...], preferred_element_type=f32)
    cols = []
    for fi in range(fold):
        block = waves[fi * n1 : (fi + 1) * n1] * scale_ref[0, step * fold + fi]
        re, im = block[:, :lanes], block[:, lanes:]
        cols.append(
            jnp.concatenate([re * tc - im * ts, im * tc + re * ts], axis=0).astype(bf16)
        )
    out = jnp.dot(v1_ref[...], jnp.concatenate(cols, axis=1), preferred_element_type=f32)
    for ri in range(2):
        for p in range(parts):
            r0 = (ri * parts + p) * devices
            piece = jnp.stack(
                [out[r0 : r0 + devices, fi * lanes : (fi + 1) * lanes] for fi in range(fold)]
            )
            o_ref[:, ri * fold : (ri + 1) * fold, p * lanes : (p + 1) * lanes] = jnp.swapaxes(
                piece, 0, 1
            ).astype(bf16)


def filter_fused(gathered, edges, scale, fold):
    devices, rows, channels = gathered.shape
    tables = filter_tables(devices * channels, devices, channels // lanes)
    whole = [pl.BlockSpec(t.shape, lambda i, n=t.ndim: (0,) * n) for t in tables]
    block = pl.BlockSpec((devices, 2 * fold, channels), lambda i: (0, i, 0))
    smem = pl.BlockSpec(memory_space=pltpu.SMEM)
    return pl.pallas_call(
        functools.partial(filter_kernel, fold),
        out_shape=jax.ShapeDtypeStruct(gathered.shape, bf16),
        grid=(rows // (2 * fold),),
        in_specs=[smem, smem, block] + whole,
        out_specs=block,
        compiler_params=pltpu.CompilerParams(vmem_limit_bytes=vmem_limit),
        name="fan_filter",
    )(edges, scale, gathered, *tables)


def filter_plain(gathered, edges, scale, fold):
    devices, rows, channels = gathered.shape
    full_count = devices * channels
    values = gathered.reshape(devices, rows // (2 * fold), 2, fold, channels)
    values = values.transpose(2, 1, 3, 0, 4).reshape(2, rows // 2, devices, channels)
    d, m = np.arange(devices), np.arange(channels)
    ad = 2.0 * np.pi * (d[:, None] * d[None, :] % devices) / devices
    am = 2.0 * np.pi * (m[:, None] * m[None, :] % channels) / channels
    at = 2.0 * np.pi * (d[:, None] * m[None, :]) / full_count
    wave = d[:, None] + devices * m[None, :]
    magnitude = jnp.asarray(np.minimum(wave, full_count - wave), jnp.int32)[None]

    def turn(layout, angle, pair, sign):
        c, s = jnp.asarray(np.cos(angle), f32), jnp.asarray(sign * np.sin(angle), f32)
        ein = functools.partial(jnp.einsum, layout, precision=highest)
        return ein(c, pair[0]) - ein(s, pair[1]), ein(c, pair[1]) + ein(s, pair[0])

    def twist(pair, sign):
        c, s = jnp.asarray(np.cos(at), f32), jnp.asarray(sign * np.sin(at), f32)
        return c * pair[0] - s * pair[1], c * pair[1] + s * pair[0]

    pair = (values[0].astype(f32), values[1].astype(f32))
    pair = twist(turn("kp,fpm->fkm", ad, pair, -1.0), -1.0)
    pair = turn("mn,fkm->fkn", am, pair, -1.0)
    passing = (magnitude >= edges[0][:, None, None]) & (magnitude <= edges[1][:, None, None])
    pair = tuple(jnp.where(passing, part, 0.0) for part in pair)
    pair = twist(turn("mn,fkn->fkm", am, pair, 1.0), 1.0)
    pair = turn("kp,fkm->fpm", ad, pair, 1.0)
    out = (jnp.stack(pair) * scale[0][None, :, None, None]).astype(bf16)
    out = out.reshape(2, rows // (2 * fold), fold, devices, channels).transpose(3, 1, 0, 2, 4)
    return out.reshape(devices, rows, channels)


def coefficient_kernel(b_ref, f_ref, cos_ref, sin_ref, out_ref):
    sums = lax.dot_general(
        b_ref[0], f_ref[...], (((1,), (1,)), ((), ())), preferred_element_type=f32
    )
    out_ref[0, 0:1, :] = jnp.sum(sums * cos_ref[...], axis=0, keepdims=True)
    out_ref[0, 1:2, :] = jnp.sum(sums * sin_ref[...], axis=0, keepdims=True)


def coefficient_spectra(turned, filtered, readings, fold):
    rank, taps, channels = turned.shape
    rows = filtered.shape[0]
    bins = row_bins(rows // 2, fold)
    angle = 2.0 * np.pi * (np.arange(taps)[:, None] * bins[None, :] % readings) / readings
    whole = lambda i: (0, 0)
    products = pl.pallas_call(
        coefficient_kernel,
        out_shape=jax.ShapeDtypeStruct((rank, 2, rows), f32),
        grid=(rank,),
        in_specs=[
            pl.BlockSpec((1, taps, channels), lambda i: (i, 0, 0)),
            pl.BlockSpec(filtered.shape, whole),
            pl.BlockSpec(angle.shape, whole),
            pl.BlockSpec(angle.shape, whole),
        ],
        out_specs=pl.BlockSpec((1, 2, rows), lambda i: (i, 0, 0)),
        compiler_params=pltpu.CompilerParams(vmem_limit_bytes=vmem_limit),
        name="coefficient_spectra",
    )(turned, filtered, jnp.asarray(np.cos(angle), f32), jnp.asarray(np.sin(angle), f32))
    parts = products.reshape(rank, 2, rows // (2 * fold), 2, fold)
    real = parts[:, 0, :, 0] - parts[:, 1, :, 1]
    imag = parts[:, 1, :, 0] + parts[:, 0, :, 1]
    return jnp.stack([real, imag], axis=2).reshape(rank, rows)


def lag_series(spectra, table):
    rank = spectra.shape[0]
    count, width = table.shape[1], table.shape[2] // 2
    high = spectra.astype(bf16)
    low = (spectra - high.astype(f32)).astype(bf16)
    both = jnp.stack([high, low]).reshape(2 * rank, half, count)
    z = jnp.einsum("rgk,gkb->grb", both, table, preferred_element_type=f32)
    z = z[:, :rank] + z[:, rank:]
    zr, zs = z[:, :, :width], z[:, :, width:]
    even = even_parts(zr[0], zs[0], [zr[g] for g in range(1, half)])
    odd = odd_parts([zs[g] for g in range(1, half)])
    series = [even[0]]
    series += [even[a] + odd[a - 1] for a in range(1, half)]
    series += [even[half]]
    series += [even[a] - odd[a - 1] for a in range(half - 1, 0, -1)]
    return jnp.concatenate(series, axis=1)


def local(waveforms, basis, bounds):
    devices = lax.axis_size("chan")
    position = lax.axis_index("chan")
    channels, readings = waveforms.shape
    rank, _, taps = basis.shape
    frequencies = bounds.shape[1]
    full_count = channels * devices
    bin_count = frequencies // devices
    fold = math.gcd(16, bin_count)
    lag_count = readings // devices

    table = jnp.asarray(time_table(frequencies, readings, fold), bf16)
    spectrum = time_spectrum(waveforms, table)
    gathered = lax.all_to_all(spectrum, "chan", split_axis=0, concat_axis=0, tiled=True)

    flat = basis.reshape(rank, channels * taps)
    gram_part = jnp.einsum("ka,ja->kj", flat, flat, preferred_element_type=f32)
    gram = jnp.sum(lax.all_gather(gram_part, "chan"), axis=0)
    factor = jnp.linalg.cholesky(gram)
    inverse = jax.scipy.linalg.cho_solve((factor, True), jnp.eye(rank, dtype=f32))
    turned = jnp.swapaxes(basis, 1, 2)

    order = bin_order(frequencies)[0].reshape(-1)
    edges = lax.dynamic_slice_in_dim(bounds[:, order], position * bin_count, bin_count, 1)
    scale = jnp.asarray(np.where(order == 0, 0.5, 1.0) / full_count, f32).reshape(1, -1)
    scale = lax.dynamic_slice_in_dim(scale, position * bin_count, bin_count, 1)
    gathered = gathered.reshape(devices, 2 * bin_count, channels)
    apply = filter_fused if channels % lanes == 0 else filter_plain
    passed = apply(gathered, edges, scale, fold).reshape(2 * frequencies, channels)
    filtered = lax.all_to_all(passed, "chan", split_axis=0, concat_axis=0, tiled=True)

    power = time_power(filtered, table)
    extended = jnp.concatenate([power, power[:taps]])
    windows = jnp.stack(
        [extended[d * lag_count : (d + 1) * lag_count + taps] for d in range(devices)]
    )
    windows = jnp.sum(
        lax.all_to_all(windows, "chan", split_axis=0, concat_axis=0, tiled=True),
        axis=0,
        keepdims=True,
    )
    spectra = coefficient_spectra(turned, filtered, readings, fold)
    series = lag_series(spectra, table)
    series = series.reshape(rank, devices, lag_count).transpose(1, 0, 2)
    series = lax.all_to_all(series, "chan", split_axis=0, concat_axis=0, tiled=True)
    correlation = jnp.sum(series, axis=0) * (2.0 / readings)

    lag = np.arange(lag_count + taps)[:, None] - np.arange(lag_count)[None, :]
    band = jnp.asarray((lag >= 0) & (lag < taps), f32)
    energy = jnp.dot(windows, band, precision=highest)[0] * (2.0 / readings) ** 2
    level = energy / (full_count * taps) + 1e-06
    solved = jnp.dot(inverse, correlation, precision=highest)
    detection = jnp.sum(correlation * solved, axis=0) / (rank * level)
    coefficients = correlation / jnp.sqrt(level)[None, :]
    return (detection, coefficients)


def solution(mesh):
    in_specs = (P("chan", "groups"), P(None, "chan", None), P())
    out_specs = (P(("groups", "chan")), P(None, ("groups", "chan")))
    return jax.shard_map(local, mesh=mesh, in_specs=in_specs, out_specs=out_specs, check_vma=False)
```

```python
import functools
import math

import jax
import jax.numpy as jnp
import numpy as np
from jax import lax
from jax.experimental import pallas as pl
from jax.experimental.pallas import tpu as pltpu
from jax.sharding import PartitionSpec as P

radix = 12
half = radix // 2
lanes = 128
highest = lax.Precision.HIGHEST
bf16 = jnp.bfloat16
f32 = jnp.float32
vmem_limit = 60 * 1024 * 1024


def even_parts(x0, x6, s):
    r = math.sqrt(3.0) / 2.0
    s1, s2, s3, s4, s5 = s
    u, v = x0 + x6, x0 - x6
    e24, d24, e15, d15 = s2 + s4, s2 - s4, s1 + s5, s1 - s5
    even0, odd0 = u + e24, e15 + s3
    even1, odd1 = v + 0.5 * d24, r * d15
    even2, odd2 = u - 0.5 * e24, 0.5 * e15 - s3
    return (
        even0 + odd0,
        even1 + odd1,
        even2 + odd2,
        v - d24,
        even2 - odd2,
        even1 - odd1,
        even0 - odd0,
    )


def odd_parts(d):
    r = math.sqrt(3.0) / 2.0
    d1, d2, d3, d4, d5 = d
    e15, m15 = d1 + d5, d1 - d5
    odd1, even1 = 0.5 * e15 + d3, r * (d2 + d4)
    odd2, even2 = r * m15, r * (d2 - d4)
    return (odd1 + even1, odd2 + even2, e15 - d3, odd2 - even2, odd1 - even1)


def bin_order(frequencies):
    ids = np.arange(frequencies)
    groups = [np.concatenate([ids[ids % radix == 0], ids[ids % radix == half]])]
    signs = [np.ones(frequencies // half)]
    for q in range(1, half):
        plus, minus = ids[ids % radix == q], ids[ids % radix == radix - q]
        groups.append(np.concatenate([plus, minus]))
        signs.append(np.concatenate([np.ones(len(plus)), -np.ones(len(minus))]))
    return np.stack(groups), np.stack(signs)


def time_table(frequencies, readings, fold):
    width = readings // radix
    groups, signs = bin_order(frequencies)
    theta = (groups[:, :, None] * np.arange(width)[None, None, :] % readings) * (
        2.0 * np.pi / readings
    )
    cos, sin = np.cos(theta), np.sin(theta)
    sg = signs[:, :, None]
    real = np.concatenate([cos, -sg * sin], axis=2)
    imag = np.concatenate([-sin, -sg * cos], axis=2)
    first = (groups[0] % radix == 0)[:, None]
    real[0] = np.concatenate([np.where(first, cos[0], 0), np.where(first, 0, cos[0])], axis=1)
    imag[0] = np.concatenate([np.where(first, -sin[0], 0), np.where(first, 0, -sin[0])], axis=1)
    count = groups.shape[1]
    both = np.stack([real, imag], axis=1).reshape(half, 2, count // fold, fold, 2 * width)
    return both.transpose(0, 2, 1, 3, 4).reshape(half, 2 * count, 2 * width)


def row_bins(frequencies, fold):
    order = bin_order(frequencies)[0].reshape(-1, 1, fold)
    return np.broadcast_to(order, (order.shape[0], 2, fold)).reshape(-1)


def spectrum_kernel(blocks, x_ref, table_ref, out_ref, y_ref):
    rows, readings = x_ref.shape
    width = readings // radix
    step = pl.program_id(0)

    @pl.when(step < blocks)
    def _():
        @pl.loop(0, rows // 16)
        def _(r):
            rs = pl.ds(r * 16, 16)
            ys = pl.ds(step * rows + r * 16, 16)
            for b0 in range(0, width, lanes):
                x = [
                    x_ref[rs, a * width + b0 : a * width + b0 + lanes].astype(f32)
                    for a in range(radix)
                ]
                even = even_parts(x[0], x[half], [x[a] + x[radix - a] for a in range(1, half)])
                odd = odd_parts([x[a] - x[radix - a] for a in range(1, half)])
                left = slice(b0, b0 + lanes)
                right = slice(width + b0, width + b0 + lanes)
                y_ref[0, ys, left] = even[0].astype(bf16)
                y_ref[0, ys, right] = even[half].astype(bf16)
                for q in range(1, half):
                    y_ref[q, ys, left] = even[q].astype(bf16)
                    y_ref[q, ys, right] = odd[q - 1].astype(bf16)

    @pl.when(step >= blocks)
    def _():
        out_ref[...] = lax.dot_general(
            table_ref[0],
            y_ref[step - blocks],
            (((1,), (1,)), ((), ())),
            preferred_element_type=f32,
        ).astype(bf16)


def time_spectrum(waveforms, table):
    channels, readings = waveforms.shape
    block = lanes if channels % lanes == 0 else channels
    blocks = channels // block
    count = table.shape[1]
    group = lambda i: jnp.maximum(i - blocks, 0)
    return pl.pallas_call(
        functools.partial(spectrum_kernel, blocks),
        out_shape=jax.ShapeDtypeStruct((half * count, channels), bf16),
        grid=(blocks + half,),
        in_specs=[
            pl.BlockSpec((block, readings), lambda i: (jnp.minimum(i, blocks - 1), 0)),
            pl.BlockSpec((1,) + table.shape[1:], lambda i: (group(i), 0, 0)),
        ],
        out_specs=pl.BlockSpec((count, channels), lambda i: (group(i), 0)),
        scratch_shapes=[pltpu.VMEM((half, channels, 2 * readings // radix), bf16)],
        compiler_params=pltpu.CompilerParams(vmem_limit_bytes=vmem_limit),
        name="time_spectrum",
    )(waveforms, table)


def series_parts(zr, zs):
    even = even_parts(zr[0], zs[0], zr[1:])
    odd = odd_parts(zs[1:])
    series = [even[0]]
    series += [even[a] + odd[a - 1] for a in range(1, half)]
    series += [even[half]]
    series += [even[a] - odd[a - 1] for a in range(half - 1, 0, -1)]
    return series


def series_kernel(fold, b_ref, f_ref, t_ref, cos_ref, sin_ref, power_ref, out_ref, z_ref, c_ref):
    group = pl.program_id(0)
    taps, count = cos_ref.shape
    rank = out_ref.shape[0]
    width = z_ref.shape[2] // 2
    z_ref[group] = lax.dot_general(
        f_ref[...], t_ref[0], (((0,), (0,)), ((), ())), preferred_element_type=f32
    )
    sums = lax.dot_general(
        b_ref[...], f_ref[...], (((1,), (1,)), ((), ())), preferred_element_type=f32
    )
    first, second = [], []
    for r in range(rank):
        member = sums[r * taps : (r + 1) * taps]
        first.append(jnp.sum(member * cos_ref[...], axis=0, keepdims=True))
        second.append(jnp.sum(member * sin_ref[...], axis=0, keepdims=True))
    first = jnp.concatenate(first, axis=0)
    second = jnp.concatenate(second, axis=0)
    ids = lax.broadcasted_iota(jnp.int32, first.shape, 1)
    spectra = first + jnp.where(
        (ids // fold) % 2 == 0,
        -pltpu.roll(second, count - fold, 1),
        pltpu.roll(second, fold, 1),
    )
    high = spectra.astype(bf16)
    low = (spectra - high.astype(f32)).astype(bf16)
    c_ref[group] = jnp.dot(high, t_ref[0], preferred_element_type=f32) + jnp.dot(
        low, t_ref[0], preferred_element_type=f32
    )

    @pl.when(group == half - 1)
    def _():
        power_ref[...] = jnp.zeros_like(power_ref)

        @pl.loop(0, z_ref.shape[1] // 16)
        def _(r):
            rs = pl.ds(r * 16, 16)
            for b0 in range(0, width, lanes):
                left = slice(b0, b0 + lanes)
                right = slice(width + b0, width + b0 + lanes)
                parts = series_parts(
                    [z_ref[g, rs, left] for g in range(half)],
                    [z_ref[g, rs, right] for g in range(half)],
                )
                for a, value in enumerate(parts):
                    square = value * value
                    power_ref[a, :, left] += square[:8] + square[8:]

        parts = series_parts(
            [c_ref[g, :, :width] for g in range(half)],
            [c_ref[g, :, width:] for g in range(half)],
        )
        for a, value in enumerate(parts):
            out_ref[:, a * width : (a + 1) * width] = value


def power_and_series(turned, filtered, table, readings, fold):
    rank, taps, channels = turned.shape
    rows = filtered.shape[0]
    count, width = table.shape[1], table.shape[2] // 2
    bins = row_bins(rows // 2, fold)
    angle = 2.0 * np.pi * (np.arange(taps)[:, None] * bins[None, :] % readings) / readings
    power, series = pl.pallas_call(
        functools.partial(series_kernel, fold),
        out_shape=(
            jax.ShapeDtypeStruct((radix, 8, width), f32),
            jax.ShapeDtypeStruct((rank, readings), f32),
        ),
        grid=(half,),
        in_specs=[
            pl.BlockSpec((rank * taps, channels), lambda i: (0, 0)),
            pl.BlockSpec((count, channels), lambda i: (i, 0)),
            pl.BlockSpec((1,) + table.shape[1:], lambda i: (i, 0, 0)),
            pl.BlockSpec((taps, count), lambda i: (0, i)),
            pl.BlockSpec((taps, count), lambda i: (0, i)),
        ],
        out_specs=(
            pl.BlockSpec((radix, 8, width), lambda i: (0, 0, 0)),
            pl.BlockSpec((rank, readings), lambda i: (0, 0)),
        ),
        scratch_shapes=[
            pltpu.VMEM((half, channels, 2 * width), f32),
            pltpu.VMEM((half, rank, 2 * width), f32),
        ],
        compiler_params=pltpu.CompilerParams(vmem_limit_bytes=vmem_limit),
        name="power_and_series",
    )(
        turned.reshape(rank * taps, channels),
        filtered,
        table,
        jnp.asarray(np.cos(angle), f32),
        jnp.asarray(np.sin(angle), f32),
    )
    return jnp.sum(power, axis=1).reshape(-1), series


def filter_tables(full_count, block_count, parts):
    n2 = lanes
    n1 = full_count // n2
    order = np.arange(n1).reshape(block_count, parts).T.reshape(-1)
    k1, k2, j = np.arange(n1), np.arange(n2), np.arange(n2)
    a1 = 2.0 * np.pi * ((k1[:, None] * order[None, :]) % n1) / n1
    a2 = 2.0 * np.pi * ((j[:, None] * k2[None, :]) % n2) / n2
    at = 2.0 * np.pi * ((k1[:, None] * j[None, :]) % full_count) / full_count
    c1, s1, c2, s2 = np.cos(a1), np.sin(a1), np.cos(a2), np.sin(a2)
    first = np.block([[c1, s1], [-s1, c1]])
    second = np.block([[c2, -s2], [s2, c2]])
    twist = np.stack([np.cos(at), np.sin(at)])
    wave = k1[:, None] + n1 * k2[None, :]
    magnitude = np.minimum(wave, full_count - wave).astype(np.int32)
    return (
        jnp.asarray(first, bf16),
        jnp.asarray(second, bf16),
        jnp.asarray(first.T.copy(), bf16),
        jnp.asarray(second.T.copy(), bf16),
        jnp.asarray(twist, f32),
        jnp.asarray(magnitude),
    )


def filter_kernel(fold, edges_ref, scale_ref, x_ref, w1_ref, w2_ref, v1_ref, v2_ref, tw_ref, mag_ref, o_ref):
    step = pl.program_id(0)
    devices = x_ref.shape[0]
    parts = x_ref.shape[2] // lanes
    n1 = mag_ref.shape[0]
    pieces = []
    for ri in range(2):
        for p in range(parts):
            piece = x_ref[:, ri * fold : (ri + 1) * fold, p * lanes : (p + 1) * lanes]
            pieces.append(jnp.swapaxes(piece.astype(f32), 0, 1).astype(bf16))
    stacked = jnp.concatenate(
        [jnp.concatenate([piece[fi] for piece in pieces], axis=0) for fi in range(fold)], axis=1
    )
    waves = jnp.dot(w1_ref[...], stacked, preferred_element_type=f32)
    tc, ts = tw_ref[0], tw_ref[1]
    rows = []
    for fi in range(fold):
        col = slice(fi * lanes, (fi + 1) * lanes)
        re, im = waves[:n1, col], waves[n1:, col]
        rows.append(
            jnp.concatenate([re * tc + im * ts, im * tc - re * ts], axis=1).astype(bf16)
        )
    waves = jnp.dot(jnp.concatenate(rows, axis=0), w2_ref[...], preferred_element_type=f32)
    mag = mag_ref[...]
    rows = []
    for fi in range(fold):
        low, high = edges_ref[0, step * fold + fi], edges_ref[1, step * fold + fi]
        passing = (mag >= low) & (mag <= high)
        block = waves[fi * n1 : (fi + 1) * n1]
        rows.append(
            jnp.concatenate(
                [
                    jnp.where(passing, block[:, :lanes], 0.0),
                    jnp.where(passing, block[:, lanes:], 0.0),
                ],
                axis=1,
            ).astype(bf16)
        )
    waves = jnp.dot(jnp.concatenate(rows, axis=0), v2_ref[...], preferred_element_type=f32)
    cols = []
    for fi in range(fold):
        block = waves[fi * n1 : (fi + 1) * n1] * scale_ref[0, step * fold + fi]
        re, im = block[:, :lanes], block[:, lanes:]
        cols.append(
            jnp.concatenate([re * tc - im * ts, im * tc + re * ts], axis=0).astype(bf16)
        )
    out = jnp.dot(v1_ref[...], jnp.concatenate(cols, axis=1), preferred_element_type=f32)
    for ri in range(2):
        for p in range(parts):
            r0 = (ri * parts + p) * devices
            piece = jnp.stack(
                [out[r0 : r0 + devices, fi * lanes : (fi + 1) * lanes] for fi in range(fold)]
            )
            o_ref[:, ri * fold : (ri + 1) * fold, p * lanes : (p + 1) * lanes] = jnp.swapaxes(
                piece, 0, 1
            ).astype(bf16)


def filter_fused(gathered, edges, scale, fold):
    devices, rows, channels = gathered.shape
    tables = filter_tables(devices * channels, devices, channels // lanes)
    whole = [pl.BlockSpec(t.shape, lambda i, n=t.ndim: (0,) * n) for t in tables]
    block = pl.BlockSpec((devices, 2 * fold, channels), lambda i: (0, i, 0))
    smem = pl.BlockSpec(memory_space=pltpu.SMEM)
    return pl.pallas_call(
        functools.partial(filter_kernel, fold),
        out_shape=jax.ShapeDtypeStruct(gathered.shape, bf16),
        grid=(rows // (2 * fold),),
        in_specs=[smem, smem, block] + whole,
        out_specs=block,
        compiler_params=pltpu.CompilerParams(vmem_limit_bytes=vmem_limit),
        name="fan_filter",
    )(edges, scale, gathered, *tables)


def filter_plain(gathered, edges, scale, fold):
    devices, rows, channels = gathered.shape
    full_count = devices * channels
    values = gathered.reshape(devices, rows // (2 * fold), 2, fold, channels)
    values = values.transpose(2, 1, 3, 0, 4).reshape(2, rows // 2, devices, channels)
    d, m = np.arange(devices), np.arange(channels)
    ad = 2.0 * np.pi * (d[:, None] * d[None, :] % devices) / devices
    am = 2.0 * np.pi * (m[:, None] * m[None, :] % channels) / channels
    at = 2.0 * np.pi * (d[:, None] * m[None, :]) / full_count
    wave = d[:, None] + devices * m[None, :]
    magnitude = jnp.asarray(np.minimum(wave, full_count - wave), jnp.int32)[None]

    def turn(layout, angle, pair, sign):
        c, s = jnp.asarray(np.cos(angle), f32), jnp.asarray(sign * np.sin(angle), f32)
        ein = functools.partial(jnp.einsum, layout, precision=highest)
        return ein(c, pair[0]) - ein(s, pair[1]), ein(c, pair[1]) + ein(s, pair[0])

    def twist(pair, sign):
        c, s = jnp.asarray(np.cos(at), f32), jnp.asarray(sign * np.sin(at), f32)
        return c * pair[0] - s * pair[1], c * pair[1] + s * pair[0]

    pair = (values[0].astype(f32), values[1].astype(f32))
    pair = twist(turn("kp,fpm->fkm", ad, pair, -1.0), -1.0)
    pair = turn("mn,fkm->fkn", am, pair, -1.0)
    passing = (magnitude >= edges[0][:, None, None]) & (magnitude <= edges[1][:, None, None])
    pair = tuple(jnp.where(passing, part, 0.0) for part in pair)
    pair = twist(turn("mn,fkn->fkm", am, pair, 1.0), 1.0)
    pair = turn("kp,fkm->fpm", ad, pair, 1.0)
    out = (jnp.stack(pair) * scale[0][None, :, None, None]).astype(bf16)
    out = out.reshape(2, rows // (2 * fold), fold, devices, channels).transpose(3, 1, 0, 2, 4)
    return out.reshape(devices, rows, channels)


def final_kernel(full_count, taps, readings, got_ref, win_ref, gram_ref, det_ref, coef_ref):
    lag_count = det_ref.shape[1]
    rank = coef_ref.shape[0]
    correlation = jnp.sum(got_ref[:, :rank, :], axis=0) * (2.0 / readings)
    window = jnp.sum(win_ref[...], axis=0, keepdims=True)
    row = lax.broadcasted_iota(jnp.int32, (window.shape[1], lag_count), 0)
    lag = row - lax.broadcasted_iota(jnp.int32, row.shape, 1)
    band = jnp.where((lag >= 0) & (lag < taps), 1.0, 0.0)
    energy = jnp.dot(
        jnp.broadcast_to(window, (8, window.shape[1])), band, precision=highest
    )[:1] * (2.0 / readings) ** 2
    level = energy / (full_count * taps) + 1e-06
    gram = jnp.sum(gram_ref[...], axis=0)
    solved = correlation
    ids = lax.broadcasted_iota(jnp.int32, (rank, 1), 0)
    for k in range(rank):
        inverse = 1.0 / gram[k : k + 1, k : k + 1]
        pivot_g, pivot_c = gram[k : k + 1] * inverse, solved[k : k + 1] * inverse
        column = gram[:, k : k + 1]
        gram = jnp.where(ids == k, pivot_g, gram - column * pivot_g)
        solved = jnp.where(ids == k, pivot_c, solved - column * pivot_c)
    det_ref[...] = jnp.sum(correlation * solved, axis=0, keepdims=True) / (rank * level)
    coef_ref[...] = correlation / jnp.sqrt(level)


def local(waveforms, basis, bounds):
    devices = lax.axis_size("chan")
    position = lax.axis_index("chan")
    channels, readings = waveforms.shape
    rank, _, taps = basis.shape
    frequencies = bounds.shape[1]
    full_count = channels * devices
    bin_count = frequencies // devices
    fold = math.gcd(16, bin_count)
    lag_count = readings // devices

    table = jnp.asarray(time_table(frequencies, readings, fold), bf16)
    spectrum = time_spectrum(waveforms, table)
    gathered = lax.all_to_all(spectrum, "chan", split_axis=0, concat_axis=0, tiled=True)

    flat = basis.reshape(rank, channels * taps)
    gram = jnp.einsum("ka,ja->kj", flat, flat, preferred_element_type=f32)
    turned = jnp.swapaxes(basis, 1, 2)

    order = bin_order(frequencies)[0].reshape(-1)
    edges = lax.dynamic_slice_in_dim(bounds[:, order], position * bin_count, bin_count, 1)
    scale = jnp.asarray(np.where(order == 0, 0.5, 1.0) / full_count, f32).reshape(1, -1)
    scale = lax.dynamic_slice_in_dim(scale, position * bin_count, bin_count, 1)
    scale, gram, turned = lax.optimization_barrier((scale, gram, turned))
    gathered = gathered.reshape(devices, 2 * bin_count, channels)
    apply = filter_fused if channels % lanes == 0 else filter_plain
    passed = apply(gathered, edges, scale, fold).reshape(2 * frequencies, channels)
    filtered = lax.all_to_all(passed, "chan", split_axis=0, concat_axis=0, tiled=True)

    power, series = power_and_series(turned, filtered, table, readings, fold)
    ahead = 1 + -(-taps // lag_count)
    gram_rows = -(-rank * rank // lag_count)
    power = power.reshape(devices, lag_count)
    windows = jnp.stack([jnp.roll(power, -n, axis=0) for n in range(ahead)], axis=1)
    gram = jnp.pad(gram.reshape(-1), (0, gram_rows * lag_count - rank * rank))
    gram = jnp.broadcast_to(
        gram.reshape(1, gram_rows, lag_count), (devices, gram_rows, lag_count)
    )
    series = series.reshape(rank, devices, lag_count).transpose(1, 0, 2)
    packed = jnp.concatenate([series, windows, gram], axis=1)
    packed = lax.all_to_all(packed, "chan", split_axis=0, concat_axis=0, tiled=True)
    windows = packed[:, rank : rank + ahead].reshape(devices, ahead * lag_count)
    gram = packed[:, rank + ahead :].reshape(devices, -1)[:, : rank * rank]
    detection, coefficients = pl.pallas_call(
        functools.partial(final_kernel, full_count, taps, readings),
        out_shape=(
            jax.ShapeDtypeStruct((1, lag_count), f32),
            jax.ShapeDtypeStruct((rank, lag_count), f32),
        ),
        compiler_params=pltpu.CompilerParams(vmem_limit_bytes=vmem_limit),
        name="detect",
    )(packed, windows, gram.reshape(devices, rank, rank))
    return (detection[0], coefficients)


def solution(mesh):
    in_specs = (P("chan", "groups"), P(None, "chan", None), P())
    out_specs = (P(("groups", "chan")), P(None, ("groups", "chan")))
    return jax.shard_map(local, mesh=mesh, in_specs=in_specs, out_specs=out_specs, check_vma=False)
```

```python
import functools
import math

import jax
import jax.numpy as jnp
import numpy as np
from jax import lax
from jax.experimental import pallas as pl
from jax.experimental.pallas import tpu as pltpu
from jax.sharding import PartitionSpec as P

radix = 12
half = radix // 2
lanes = 128
highest = lax.Precision.HIGHEST
bf16 = jnp.bfloat16
f32 = jnp.float32
vmem_limit = 60 * 1024 * 1024


def even_parts(x0, x6, s):
    r = math.sqrt(3.0) / 2.0
    s1, s2, s3, s4, s5 = s
    u, v = x0 + x6, x0 - x6
    e24, d24, e15, d15 = s2 + s4, s2 - s4, s1 + s5, s1 - s5
    even0, odd0 = u + e24, e15 + s3
    even1, odd1 = v + 0.5 * d24, r * d15
    even2, odd2 = u - 0.5 * e24, 0.5 * e15 - s3
    return (
        even0 + odd0,
        even1 + odd1,
        even2 + odd2,
        v - d24,
        even2 - odd2,
        even1 - odd1,
        even0 - odd0,
    )


def odd_parts(d):
    r = math.sqrt(3.0) / 2.0
    d1, d2, d3, d4, d5 = d
    e15, m15 = d1 + d5, d1 - d5
    odd1, even1 = 0.5 * e15 + d3, r * (d2 + d4)
    odd2, even2 = r * m15, r * (d2 - d4)
    return (odd1 + even1, odd2 + even2, e15 - d3, odd2 - even2, odd1 - even1)


def bin_order(frequencies):
    ids = np.arange(frequencies)
    groups = [np.concatenate([ids[ids % radix == 0], ids[ids % radix == half]])]
    signs = [np.ones(frequencies // half)]
    for q in range(1, half):
        plus, minus = ids[ids % radix == q], ids[ids % radix == radix - q]
        groups.append(np.concatenate([plus, minus]))
        signs.append(np.concatenate([np.ones(len(plus)), -np.ones(len(minus))]))
    return np.stack(groups), np.stack(signs)


def time_table(frequencies, readings, fold):
    width = readings // radix
    groups, signs = bin_order(frequencies)
    theta = (groups[:, :, None] * np.arange(width)[None, None, :] % readings) * (
        2.0 * np.pi / readings
    )
    cos, sin = np.cos(theta), np.sin(theta)
    sg = signs[:, :, None]
    real = np.concatenate([cos, -sg * sin], axis=2)
    imag = np.concatenate([-sin, -sg * cos], axis=2)
    first = (groups[0] % radix == 0)[:, None]
    real[0] = np.concatenate([np.where(first, cos[0], 0), np.where(first, 0, cos[0])], axis=1)
    imag[0] = np.concatenate([np.where(first, -sin[0], 0), np.where(first, 0, -sin[0])], axis=1)
    count = groups.shape[1]
    both = np.stack([real, imag], axis=1).reshape(half, 2, count // fold, fold, 2 * width)
    return both.transpose(0, 2, 1, 3, 4).reshape(half, 2 * count, 2 * width)


def row_bins(frequencies, fold):
    order = bin_order(frequencies)[0].reshape(-1, 1, fold)
    return np.broadcast_to(order, (order.shape[0], 2, fold)).reshape(-1)


def spectrum_kernel(blocks, x_ref, table_ref, out_ref, y_ref):
    rows, readings = x_ref.shape
    width = readings // radix
    step = pl.program_id(0)

    @pl.when(step < blocks)
    def _():
        @pl.loop(0, rows // 16)
        def _(r):
            rs = pl.ds(r * 16, 16)
            ys = pl.ds(step * rows + r * 16, 16)
            for b0 in range(0, width, lanes):
                x = [
                    x_ref[rs, a * width + b0 : a * width + b0 + lanes].astype(f32)
                    for a in range(radix)
                ]
                even = even_parts(x[0], x[half], [x[a] + x[radix - a] for a in range(1, half)])
                odd = odd_parts([x[a] - x[radix - a] for a in range(1, half)])
                left = slice(b0, b0 + lanes)
                right = slice(width + b0, width + b0 + lanes)
                y_ref[0, ys, left] = even[0].astype(bf16)
                y_ref[0, ys, right] = even[half].astype(bf16)
                for q in range(1, half):
                    y_ref[q, ys, left] = even[q].astype(bf16)
                    y_ref[q, ys, right] = odd[q - 1].astype(bf16)

    @pl.when(step >= blocks)
    def _():
        out_ref[...] = lax.dot_general(
            table_ref[0],
            y_ref[step - blocks],
            (((1,), (1,)), ((), ())),
            preferred_element_type=f32,
        ).astype(bf16)


def time_spectrum(waveforms, table):
    channels, readings = waveforms.shape
    block = lanes if channels % lanes == 0 else channels
    blocks = channels // block
    count = table.shape[1]
    group = lambda i: jnp.maximum(i - blocks, 0)
    return pl.pallas_call(
        functools.partial(spectrum_kernel, blocks),
        out_shape=jax.ShapeDtypeStruct((half * count, channels), bf16),
        grid=(blocks + half,),
        in_specs=[
            pl.BlockSpec((block, readings), lambda i: (jnp.minimum(i, blocks - 1), 0)),
            pl.BlockSpec((1,) + table.shape[1:], lambda i: (group(i), 0, 0)),
        ],
        out_specs=pl.BlockSpec((count, channels), lambda i: (group(i), 0)),
        scratch_shapes=[pltpu.VMEM((half, channels, 2 * readings // radix), bf16)],
        compiler_params=pltpu.CompilerParams(vmem_limit_bytes=vmem_limit),
        name="time_spectrum",
    )(waveforms, table)


def series_parts(zr, zs):
    even = even_parts(zr[0], zs[0], zr[1:])
    odd = odd_parts(zs[1:])
    series = [even[0]]
    series += [even[a] + odd[a - 1] for a in range(1, half)]
    series += [even[half]]
    series += [even[a] - odd[a - 1] for a in range(half - 1, 0, -1)]
    return series


def series_kernel(fold, b_ref, f_ref, t_ref, cos_ref, sin_ref, power_ref, out_ref, z_ref, c_ref):
    group = pl.program_id(0)
    taps, count = cos_ref.shape
    rank = out_ref.shape[0]
    width = z_ref.shape[2] // 2
    z_ref[group] = lax.dot_general(
        f_ref[...], t_ref[0], (((0,), (0,)), ((), ())), preferred_element_type=f32
    )
    sums = lax.dot_general(
        b_ref[...], f_ref[...], (((1,), (1,)), ((), ())), preferred_element_type=f32
    )
    first, second = [], []
    for r in range(rank):
        member = sums[r * taps : (r + 1) * taps]
        first.append(jnp.sum(member * cos_ref[...], axis=0, keepdims=True))
        second.append(jnp.sum(member * sin_ref[...], axis=0, keepdims=True))
    first = jnp.concatenate(first, axis=0)
    second = jnp.concatenate(second, axis=0)
    ids = lax.broadcasted_iota(jnp.int32, first.shape, 1)
    spectra = first + jnp.where(
        (ids // fold) % 2 == 0,
        -pltpu.roll(second, count - fold, 1),
        pltpu.roll(second, fold, 1),
    )
    high = spectra.astype(bf16)
    low = (spectra - high.astype(f32)).astype(bf16)
    c_ref[group] = jnp.dot(high, t_ref[0], preferred_element_type=f32) + jnp.dot(
        low, t_ref[0], preferred_element_type=f32
    )

    @pl.when(group == half - 1)
    def _():
        power_ref[...] = jnp.zeros_like(power_ref)

        @pl.loop(0, z_ref.shape[1] // 16)
        def _(r):
            rs = pl.ds(r * 16, 16)
            for b0 in range(0, width, lanes):
                left = slice(b0, b0 + lanes)
                right = slice(width + b0, width + b0 + lanes)
                parts = series_parts(
                    [z_ref[g, rs, left] for g in range(half)],
                    [z_ref[g, rs, right] for g in range(half)],
                )
                for a, value in enumerate(parts):
                    square = value * value
                    power_ref[a, :, left] += square[:8] + square[8:]

        parts = series_parts(
            [c_ref[g, :, :width] for g in range(half)],
            [c_ref[g, :, width:] for g in range(half)],
        )
        for a, value in enumerate(parts):
            out_ref[:, a * width : (a + 1) * width] = value


def power_and_series(turned, filtered, table, readings, fold):
    rank, taps, channels = turned.shape
    rows = filtered.shape[0]
    count, width = table.shape[1], table.shape[2] // 2
    bins = row_bins(rows // 2, fold)
    angle = 2.0 * np.pi * (np.arange(taps)[:, None] * bins[None, :] % readings) / readings
    power, series = pl.pallas_call(
        functools.partial(series_kernel, fold),
        out_shape=(
            jax.ShapeDtypeStruct((radix, 8, width), f32),
            jax.ShapeDtypeStruct((rank, readings), f32),
        ),
        grid=(half,),
        in_specs=[
            pl.BlockSpec((rank * taps, channels), lambda i: (0, 0)),
            pl.BlockSpec((count, channels), lambda i: (i, 0)),
            pl.BlockSpec((1,) + table.shape[1:], lambda i: (i, 0, 0)),
            pl.BlockSpec((taps, count), lambda i: (0, i)),
            pl.BlockSpec((taps, count), lambda i: (0, i)),
        ],
        out_specs=(
            pl.BlockSpec((radix, 8, width), lambda i: (0, 0, 0)),
            pl.BlockSpec((rank, readings), lambda i: (0, 0)),
        ),
        scratch_shapes=[
            pltpu.VMEM((half, channels, 2 * width), f32),
            pltpu.VMEM((half, rank, 2 * width), f32),
        ],
        compiler_params=pltpu.CompilerParams(vmem_limit_bytes=vmem_limit),
        name="power_and_series",
    )(
        turned.reshape(rank * taps, channels),
        filtered,
        table,
        jnp.asarray(np.cos(angle), f32),
        jnp.asarray(np.sin(angle), f32),
    )
    return jnp.sum(power, axis=1).reshape(-1), series


def filter_tables(full_count, block_count, parts):
    n2 = lanes
    n1 = full_count // n2
    order = np.arange(n1).reshape(block_count, parts).T.reshape(-1)
    k1, k2, j = np.arange(n1), np.arange(n2), np.arange(n2)
    a1 = 2.0 * np.pi * ((k1[:, None] * order[None, :]) % n1) / n1
    a2 = 2.0 * np.pi * ((j[:, None] * k2[None, :]) % n2) / n2
    at = 2.0 * np.pi * ((k1[:, None] * j[None, :]) % full_count) / full_count
    c1, s1, c2, s2 = np.cos(a1), np.sin(a1), np.cos(a2), np.sin(a2)
    first = np.block([[c1, s1], [-s1, c1]])
    second = np.block([[c2, -s2], [s2, c2]])
    twist = np.stack([np.cos(at), np.sin(at)])
    wave = k1[:, None] + n1 * k2[None, :]
    magnitude = np.minimum(wave, full_count - wave).astype(np.int32)
    return (
        jnp.asarray(first, bf16),
        jnp.asarray(second, bf16),
        jnp.asarray(first.T.copy(), bf16),
        jnp.asarray(second.T.copy(), bf16),
        jnp.asarray(twist, f32),
        jnp.asarray(magnitude),
    )


def filter_kernel(fold, edges_ref, scale_ref, x_ref, w1_ref, w2_ref, v1_ref, v2_ref, tw_ref, mag_ref, o_ref):
    step = pl.program_id(0)
    devices = x_ref.shape[0]
    parts = x_ref.shape[2] // lanes
    n1 = mag_ref.shape[0]
    pieces = []
    for ri in range(2):
        for p in range(parts):
            piece = x_ref[:, ri * fold : (ri + 1) * fold, p * lanes : (p + 1) * lanes]
            pieces.append(jnp.swapaxes(piece.astype(f32), 0, 1).astype(bf16))
    stacked = jnp.concatenate(
        [jnp.concatenate([piece[fi] for piece in pieces], axis=0) for fi in range(fold)], axis=1
    )
    waves = jnp.dot(w1_ref[...], stacked, preferred_element_type=f32)
    tc, ts = tw_ref[0], tw_ref[1]
    rows = []
    for fi in range(fold):
        col = slice(fi * lanes, (fi + 1) * lanes)
        re, im = waves[:n1, col], waves[n1:, col]
        rows.append(
            jnp.concatenate([re * tc + im * ts, im * tc - re * ts], axis=1).astype(bf16)
        )
    waves = jnp.dot(jnp.concatenate(rows, axis=0), w2_ref[...], preferred_element_type=f32)
    mag = mag_ref[...]
    rows = []
    for fi in range(fold):
        low, high = edges_ref[0, step * fold + fi], edges_ref[1, step * fold + fi]
        passing = (mag >= low) & (mag <= high)
        block = waves[fi * n1 : (fi + 1) * n1]
        rows.append(
            jnp.concatenate(
                [
                    jnp.where(passing, block[:, :lanes], 0.0),
                    jnp.where(passing, block[:, lanes:], 0.0),
                ],
                axis=1,
            ).astype(bf16)
        )
    waves = jnp.dot(jnp.concatenate(rows, axis=0), v2_ref[...], preferred_element_type=f32)
    cols = []
    for fi in range(fold):
        block = waves[fi * n1 : (fi + 1) * n1] * scale_ref[0, step * fold + fi]
        re, im = block[:, :lanes], block[:, lanes:]
        cols.append(
            jnp.concatenate([re * tc - im * ts, im * tc + re * ts], axis=0).astype(bf16)
        )
    out = jnp.dot(v1_ref[...], jnp.concatenate(cols, axis=1), preferred_element_type=f32)
    for ri in range(2):
        for p in range(parts):
            r0 = (ri * parts + p) * devices
            piece = jnp.stack(
                [out[r0 : r0 + devices, fi * lanes : (fi + 1) * lanes] for fi in range(fold)]
            )
            o_ref[:, ri * fold : (ri + 1) * fold, p * lanes : (p + 1) * lanes] = jnp.swapaxes(
                piece, 0, 1
            ).astype(bf16)


def filter_fused(gathered, edges, scale, fold):
    devices, rows, channels = gathered.shape
    tables = filter_tables(devices * channels, devices, channels // lanes)
    whole = [pl.BlockSpec(t.shape, lambda i, n=t.ndim: (0,) * n) for t in tables]
    block = pl.BlockSpec((devices, 2 * fold, channels), lambda i: (0, i, 0))
    smem = pl.BlockSpec(memory_space=pltpu.SMEM)
    return pl.pallas_call(
        functools.partial(filter_kernel, fold),
        out_shape=jax.ShapeDtypeStruct(gathered.shape, bf16),
        grid=(rows // (2 * fold),),
        in_specs=[smem, smem, block] + whole,
        out_specs=block,
        compiler_params=pltpu.CompilerParams(vmem_limit_bytes=vmem_limit),
        name="fan_filter",
    )(edges, scale, gathered, *tables)


def filter_plain(gathered, edges, scale, fold):
    devices, rows, channels = gathered.shape
    full_count = devices * channels
    values = gathered.reshape(devices, rows // (2 * fold), 2, fold, channels)
    values = values.transpose(2, 1, 3, 0, 4).reshape(2, rows // 2, devices, channels)
    d, m = np.arange(devices), np.arange(channels)
    ad = 2.0 * np.pi * (d[:, None] * d[None, :] % devices) / devices
    am = 2.0 * np.pi * (m[:, None] * m[None, :] % channels) / channels
    at = 2.0 * np.pi * (d[:, None] * m[None, :]) / full_count
    wave = d[:, None] + devices * m[None, :]
    magnitude = jnp.asarray(np.minimum(wave, full_count - wave), jnp.int32)[None]

    def turn(layout, angle, pair, sign):
        c, s = jnp.asarray(np.cos(angle), f32), jnp.asarray(sign * np.sin(angle), f32)
        ein = functools.partial(jnp.einsum, layout, precision=highest)
        return ein(c, pair[0]) - ein(s, pair[1]), ein(c, pair[1]) + ein(s, pair[0])

    def twist(pair, sign):
        c, s = jnp.asarray(np.cos(at), f32), jnp.asarray(sign * np.sin(at), f32)
        return c * pair[0] - s * pair[1], c * pair[1] + s * pair[0]

    pair = (values[0].astype(f32), values[1].astype(f32))
    pair = twist(turn("kp,fpm->fkm", ad, pair, -1.0), -1.0)
    pair = turn("mn,fkm->fkn", am, pair, -1.0)
    passing = (magnitude >= edges[0][:, None, None]) & (magnitude <= edges[1][:, None, None])
    pair = tuple(jnp.where(passing, part, 0.0) for part in pair)
    pair = twist(turn("mn,fkn->fkm", am, pair, 1.0), 1.0)
    pair = turn("kp,fkm->fpm", ad, pair, 1.0)
    out = (jnp.stack(pair) * scale[0][None, :, None, None]).astype(bf16)
    out = out.reshape(2, rows // (2 * fold), fold, devices, channels).transpose(3, 1, 0, 2, 4)
    return out.reshape(devices, rows, channels)


def greet(me, devices):
    barrier = pltpu.get_barrier_semaphore()

    @pl.loop(1, devices)
    def _(off):
        pl.semaphore_signal(barrier, inc=1, device_id={"chan": lax.rem(me + off, devices)})

    pl.semaphore_wait(barrier, devices - 1)


def final_kernel(
    full_count, taps, readings, series_ref, extra_ref, det_ref, coef_ref, got_ref, more_ref, sent, came
):
    devices, rank, lag_count = series_ref.shape
    square = rank * rank
    span = extra_ref.shape[2] - square
    me = lax.axis_index("chan")
    greet(me, devices)

    def copies(peer, slot):
        pair = ((series_ref, got_ref), (extra_ref, more_ref))
        return [
            pltpu.make_async_remote_copy(
                src_ref=src.at[peer],
                dst_ref=dst.at[slot],
                send_sem=sent.at[n, peer],
                recv_sem=came.at[n, slot],
                device_id={"chan": peer},
            )
            for n, (src, dst) in enumerate(pair)
        ]

    @pl.loop(1, devices)
    def _(off):
        for copy in copies(lax.rem(me + off, devices), me):
            copy.start()

    got_ref[me] = series_ref[me]
    more_ref[me] = extra_ref[me]

    @pl.loop(1, devices)
    def _(off):
        peer = lax.rem(me + off, devices)
        for copy in copies(peer, peer):
            copy.wait()

    correlation = jnp.sum(got_ref[...].astype(f32), axis=0) * (2.0 / readings)
    extra = jnp.sum(more_ref[...], axis=0)
    window = extra[:, :span]
    packed = jnp.broadcast_to(extra[:, span:], (rank, square))
    spread = lax.broadcasted_iota(jnp.int32, packed.shape, 1)
    packed = jnp.where(
        spread // rank == lax.broadcasted_iota(jnp.int32, packed.shape, 0), packed, 0.0
    )
    pick = lax.broadcasted_iota(jnp.int32, (square, rank), 0) % rank
    pick = jnp.where(pick == lax.broadcasted_iota(jnp.int32, pick.shape, 1), 1.0, 0.0)
    gram = jnp.dot(packed, pick, precision=highest)
    row = lax.broadcasted_iota(jnp.int32, (window.shape[1], lag_count), 0)
    lag = row - lax.broadcasted_iota(jnp.int32, row.shape, 1)
    band = jnp.where((lag >= 0) & (lag < taps), 1.0, 0.0)
    energy = jnp.dot(
        jnp.broadcast_to(window, (8, window.shape[1])), band, precision=highest
    )[:1] * (2.0 / readings) ** 2
    level = energy / (full_count * taps) + 1e-06
    solved = correlation
    ids = lax.broadcasted_iota(jnp.int32, (rank, 1), 0)
    for k in range(rank):
        inverse = 1.0 / gram[k : k + 1, k : k + 1]
        pivot_g, pivot_c = gram[k : k + 1] * inverse, solved[k : k + 1] * inverse
        column = gram[:, k : k + 1]
        gram = jnp.where(ids == k, pivot_g, gram - column * pivot_g)
        solved = jnp.where(ids == k, pivot_c, solved - column * pivot_c)
    det_ref[...] = jnp.sum(correlation * solved, axis=0, keepdims=True) / (rank * level)
    coef_ref[...] = correlation / jnp.sqrt(level)


def local(waveforms, basis, bounds):
    devices = lax.axis_size("chan")
    position = lax.axis_index("chan")
    channels, readings = waveforms.shape
    rank, _, taps = basis.shape
    frequencies = bounds.shape[1]
    full_count = channels * devices
    bin_count = frequencies // devices
    fold = math.gcd(16, bin_count)
    lag_count = readings // devices

    table = jnp.asarray(time_table(frequencies, readings, fold), bf16)
    spectrum = time_spectrum(waveforms, table)
    gathered = lax.all_to_all(spectrum, "chan", split_axis=0, concat_axis=0, tiled=True)

    flat = basis.reshape(rank, channels * taps)
    gram = jnp.einsum("ka,ja->kj", flat, flat, preferred_element_type=f32)
    turned = jnp.swapaxes(basis, 1, 2)

    order = bin_order(frequencies)[0].reshape(-1)
    edges = lax.dynamic_slice_in_dim(bounds[:, order], position * bin_count, bin_count, 1)
    scale = jnp.asarray(np.where(order == 0, 0.5, 1.0) / full_count, f32).reshape(1, -1)
    scale = lax.dynamic_slice_in_dim(scale, position * bin_count, bin_count, 1)
    scale, gram, turned = lax.optimization_barrier((scale, gram, turned))
    gathered = gathered.reshape(devices, 2 * bin_count, channels)
    apply = filter_fused if channels % lanes == 0 else filter_plain
    passed = apply(gathered, edges, scale, fold).reshape(2 * frequencies, channels)
    filtered = lax.all_to_all(passed, "chan", split_axis=0, concat_axis=0, tiled=True)

    power, series = power_and_series(turned, filtered, table, readings, fold)
    ahead = 1 + -(-taps // lag_count)
    span = -(-(lag_count + taps) // lanes) * lanes
    power = power.reshape(devices, lag_count)
    windows = jnp.concatenate([jnp.roll(power, -n, axis=0) for n in range(ahead)], axis=1)
    windows = jnp.pad(windows[:, : lag_count + taps], ((0, 0), (0, span - lag_count - taps)))
    gram = jnp.broadcast_to(gram.reshape(1, -1), (devices, rank * rank))
    extra = jnp.concatenate([windows, gram], axis=1)[:, None, :]
    series = series.astype(bf16).reshape(rank, devices, lag_count).transpose(1, 0, 2)
    vmem = pl.BlockSpec(memory_space=pltpu.VMEM)
    detection, coefficients = pl.pallas_call(
        functools.partial(final_kernel, full_count, taps, readings),
        out_shape=(
            jax.ShapeDtypeStruct((1, lag_count), f32),
            jax.ShapeDtypeStruct((rank, lag_count), f32),
        ),
        in_specs=[vmem, vmem],
        out_specs=(vmem, vmem),
        scratch_shapes=[
            pltpu.VMEM(series.shape, bf16),
            pltpu.VMEM(extra.shape, f32),
            pltpu.SemaphoreType.DMA((2, devices)),
            pltpu.SemaphoreType.DMA((2, devices)),
        ],
        compiler_params=pltpu.CompilerParams(
            vmem_limit_bytes=vmem_limit, collective_id=0, has_side_effects=True
        ),
        name="detect",
    )(series, extra)
    return (detection[0], coefficients)


def solution(mesh):
    in_specs = (P("chan", "groups"), P(None, "chan", None), P())
    out_specs = (P(("groups", "chan")), P(None, ("groups", "chan")))
    return jax.shard_map(local, mesh=mesh, in_specs=in_specs, out_specs=out_specs, check_vma=False)
```

```python
import functools
import math

import jax
import jax.numpy as jnp
import numpy as np
from jax import lax
from jax.experimental import pallas as pl
from jax.experimental.pallas import tpu as pltpu
from jax.sharding import PartitionSpec as P

radix = 12
half = radix // 2
lanes = 128
highest = lax.Precision.HIGHEST
bf16 = jnp.bfloat16
f32 = jnp.float32
vmem_limit = 60 * 1024 * 1024


def even_parts(x0, x6, s):
    r = math.sqrt(3.0) / 2.0
    s1, s2, s3, s4, s5 = s
    u, v = x0 + x6, x0 - x6
    e24, d24, e15, d15 = s2 + s4, s2 - s4, s1 + s5, s1 - s5
    even0, odd0 = u + e24, e15 + s3
    even1, odd1 = v + 0.5 * d24, r * d15
    even2, odd2 = u - 0.5 * e24, 0.5 * e15 - s3
    return (
        even0 + odd0,
        even1 + odd1,
        even2 + odd2,
        v - d24,
        even2 - odd2,
        even1 - odd1,
        even0 - odd0,
    )


def odd_parts(d):
    r = math.sqrt(3.0) / 2.0
    d1, d2, d3, d4, d5 = d
    e15, m15 = d1 + d5, d1 - d5
    odd1, even1 = 0.5 * e15 + d3, r * (d2 + d4)
    odd2, even2 = r * m15, r * (d2 - d4)
    return (odd1 + even1, odd2 + even2, e15 - d3, odd2 - even2, odd1 - even1)


def bin_order(frequencies):
    ids = np.arange(frequencies)
    groups = [np.concatenate([ids[ids % radix == 0], ids[ids % radix == half]])]
    signs = [np.ones(frequencies // half)]
    for q in range(1, half):
        plus, minus = ids[ids % radix == q], ids[ids % radix == radix - q]
        groups.append(np.concatenate([plus, minus]))
        signs.append(np.concatenate([np.ones(len(plus)), -np.ones(len(minus))]))
    return np.stack(groups), np.stack(signs)


def time_table(frequencies, readings, fold):
    width = readings // radix
    groups, signs = bin_order(frequencies)
    theta = (groups[:, :, None] * np.arange(width)[None, None, :] % readings) * (
        2.0 * np.pi / readings
    )
    cos, sin = np.cos(theta), np.sin(theta)
    sg = signs[:, :, None]
    real = np.concatenate([cos, -sg * sin], axis=2)
    imag = np.concatenate([-sin, -sg * cos], axis=2)
    first = (groups[0] % radix == 0)[:, None]
    real[0] = np.concatenate([np.where(first, cos[0], 0), np.where(first, 0, cos[0])], axis=1)
    imag[0] = np.concatenate([np.where(first, -sin[0], 0), np.where(first, 0, -sin[0])], axis=1)
    count = groups.shape[1]
    both = np.stack([real, imag], axis=1).reshape(half, 2, count // fold, fold, 2 * width)
    return both.transpose(0, 2, 1, 3, 4).reshape(half, 2 * count, 2 * width)


def row_bins(frequencies, fold):
    order = bin_order(frequencies)[0].reshape(-1, 1, fold)
    return np.broadcast_to(order, (order.shape[0], 2, fold)).reshape(-1)


def spectrum_kernel(blocks, x_ref, table_ref, out_ref, y_ref):
    rows, readings = x_ref.shape
    width = readings // radix
    step = pl.program_id(0)

    @pl.when(step < blocks)
    def _():
        @pl.loop(0, rows // 16)
        def _(r):
            rs = pl.ds(r * 16, 16)
            ys = pl.ds(step * rows + r * 16, 16)
            for b0 in range(0, width, lanes):
                x = [
                    x_ref[rs, a * width + b0 : a * width + b0 + lanes].astype(f32)
                    for a in range(radix)
                ]
                even = even_parts(x[0], x[half], [x[a] + x[radix - a] for a in range(1, half)])
                odd = odd_parts([x[a] - x[radix - a] for a in range(1, half)])
                left = slice(b0, b0 + lanes)
                right = slice(width + b0, width + b0 + lanes)
                y_ref[0, ys, left] = even[0].astype(bf16)
                y_ref[0, ys, right] = even[half].astype(bf16)
                for q in range(1, half):
                    y_ref[q, ys, left] = even[q].astype(bf16)
                    y_ref[q, ys, right] = odd[q - 1].astype(bf16)

    @pl.when(step >= blocks)
    def _():
        out_ref[...] = lax.dot_general(
            table_ref[0],
            y_ref[step - blocks],
            (((1,), (1,)), ((), ())),
            preferred_element_type=f32,
        ).astype(bf16)


def time_spectrum(waveforms, table):
    channels, readings = waveforms.shape
    block = lanes if channels % lanes == 0 else channels
    blocks = channels // block
    count = table.shape[1]
    group = lambda i: jnp.maximum(i - blocks, 0)
    return pl.pallas_call(
        functools.partial(spectrum_kernel, blocks),
        out_shape=jax.ShapeDtypeStruct((half * count, channels), bf16),
        grid=(blocks + half,),
        in_specs=[
            pl.BlockSpec((block, readings), lambda i: (jnp.minimum(i, blocks - 1), 0)),
            pl.BlockSpec((1,) + table.shape[1:], lambda i: (group(i), 0, 0)),
        ],
        out_specs=pl.BlockSpec((count, channels), lambda i: (group(i), 0)),
        scratch_shapes=[pltpu.VMEM((half, channels, 2 * readings // radix), bf16)],
        compiler_params=pltpu.CompilerParams(vmem_limit_bytes=vmem_limit),
        name="time_spectrum",
    )(waveforms, table)


def series_parts(zr, zs):
    even = even_parts(zr[0], zs[0], zr[1:])
    odd = odd_parts(zs[1:])
    series = [even[0]]
    series += [even[a] + odd[a - 1] for a in range(1, half)]
    series += [even[half]]
    series += [even[a] - odd[a - 1] for a in range(half - 1, 0, -1)]
    return series


def series_kernel(fold, b_ref, f_ref, t_ref, cos_ref, sin_ref, power_ref, out_ref, z_ref, c_ref):
    group = pl.program_id(0)
    taps, count = cos_ref.shape
    rank = out_ref.shape[0]
    width = z_ref.shape[2] // 2
    z_ref[group] = lax.dot_general(
        f_ref[...], t_ref[0], (((0,), (0,)), ((), ())), preferred_element_type=f32
    )
    sums = lax.dot_general(
        b_ref[...], f_ref[...], (((1,), (1,)), ((), ())), preferred_element_type=f32
    )
    first, second = [], []
    for r in range(rank):
        member = sums[r * taps : (r + 1) * taps]
        first.append(jnp.sum(member * cos_ref[...], axis=0, keepdims=True))
        second.append(jnp.sum(member * sin_ref[...], axis=0, keepdims=True))
    first = jnp.concatenate(first, axis=0)
    second = jnp.concatenate(second, axis=0)
    ids = lax.broadcasted_iota(jnp.int32, first.shape, 1)
    spectra = first + jnp.where(
        (ids // fold) % 2 == 0,
        -pltpu.roll(second, count - fold, 1),
        pltpu.roll(second, fold, 1),
    )
    high = spectra.astype(bf16)
    low = (spectra - high.astype(f32)).astype(bf16)
    c_ref[group] = jnp.dot(high, t_ref[0], preferred_element_type=f32) + jnp.dot(
        low, t_ref[0], preferred_element_type=f32
    )

    @pl.when(group == half - 1)
    def _():
        power_ref[...] = jnp.zeros_like(power_ref)

        @pl.loop(0, z_ref.shape[1] // 16)
        def _(r):
            rs = pl.ds(r * 16, 16)
            for b0 in range(0, width, lanes):
                left = slice(b0, b0 + lanes)
                right = slice(width + b0, width + b0 + lanes)
                parts = series_parts(
                    [z_ref[g, rs, left] for g in range(half)],
                    [z_ref[g, rs, right] for g in range(half)],
                )
                for a, value in enumerate(parts):
                    square = value * value
                    power_ref[a, :, left] += square[:8] + square[8:]

        parts = series_parts(
            [c_ref[g, :, :width] for g in range(half)],
            [c_ref[g, :, width:] for g in range(half)],
        )
        for a, value in enumerate(parts):
            out_ref[:, a * width : (a + 1) * width] = value


def power_and_series(turned, filtered, table, readings, fold):
    rank, taps, channels = turned.shape
    rows = filtered.shape[0]
    count, width = table.shape[1], table.shape[2] // 2
    bins = row_bins(rows // 2, fold)
    angle = 2.0 * np.pi * (np.arange(taps)[:, None] * bins[None, :] % readings) / readings
    power, series = pl.pallas_call(
        functools.partial(series_kernel, fold),
        out_shape=(
            jax.ShapeDtypeStruct((radix, 8, width), f32),
            jax.ShapeDtypeStruct((rank, readings), f32),
        ),
        grid=(half,),
        in_specs=[
            pl.BlockSpec((rank * taps, channels), lambda i: (0, 0)),
            pl.BlockSpec((count, channels), lambda i: (i, 0)),
            pl.BlockSpec((1,) + table.shape[1:], lambda i: (i, 0, 0)),
            pl.BlockSpec((taps, count), lambda i: (0, i)),
            pl.BlockSpec((taps, count), lambda i: (0, i)),
        ],
        out_specs=(
            pl.BlockSpec((radix, 8, width), lambda i: (0, 0, 0)),
            pl.BlockSpec((rank, readings), lambda i: (0, 0)),
        ),
        scratch_shapes=[
            pltpu.VMEM((half, channels, 2 * width), f32),
            pltpu.VMEM((half, rank, 2 * width), f32),
        ],
        compiler_params=pltpu.CompilerParams(vmem_limit_bytes=vmem_limit),
        name="power_and_series",
    )(
        turned.reshape(rank * taps, channels),
        filtered,
        table,
        jnp.asarray(np.cos(angle), f32),
        jnp.asarray(np.sin(angle), f32),
    )
    return jnp.sum(power, axis=1).reshape(-1), series


def filter_tables(full_count, block_count, parts):
    n2 = lanes
    n1 = full_count // n2
    order = np.arange(n1).reshape(block_count, parts).T.reshape(-1)
    k1, k2, j = np.arange(n1), np.arange(n2), np.arange(n2)
    a1 = 2.0 * np.pi * ((k1[:, None] * order[None, :]) % n1) / n1
    a2 = 2.0 * np.pi * ((j[:, None] * k2[None, :]) % n2) / n2
    at = 2.0 * np.pi * ((k1[:, None] * j[None, :]) % full_count) / full_count
    c1, s1, c2, s2 = np.cos(a1), np.sin(a1), np.cos(a2), np.sin(a2)
    first = np.block([[c1, s1], [-s1, c1]])
    second = np.block([[c2, -s2], [s2, c2]])
    twist = np.stack([np.cos(at), np.sin(at)])
    wave = k1[:, None] + n1 * k2[None, :]
    magnitude = np.minimum(wave, full_count - wave).astype(np.int32)
    return (
        jnp.asarray(first, bf16),
        jnp.asarray(second, bf16),
        jnp.asarray(first.T.copy(), bf16),
        jnp.asarray(second.T.copy(), bf16),
        jnp.asarray(twist, f32),
        jnp.asarray(magnitude),
    )


def filter_chunk(fold, step, edges_ref, scale_ref, x_ref, w1_ref, w2_ref, v1_ref, v2_ref, tw_ref, mag_ref, o_ref):
    devices = x_ref.shape[0]
    parts = x_ref.shape[2] // lanes
    n1 = mag_ref.shape[0]
    pieces = []
    for ri in range(2):
        for p in range(parts):
            piece = x_ref[:, ri * fold : (ri + 1) * fold, p * lanes : (p + 1) * lanes]
            pieces.append(jnp.swapaxes(piece.astype(f32), 0, 1).astype(bf16))
    stacked = jnp.concatenate(
        [jnp.concatenate([piece[fi] for piece in pieces], axis=0) for fi in range(fold)], axis=1
    )
    waves = jnp.dot(w1_ref[...], stacked, preferred_element_type=f32)
    tc, ts = tw_ref[0], tw_ref[1]
    rows = []
    for fi in range(fold):
        col = slice(fi * lanes, (fi + 1) * lanes)
        re, im = waves[:n1, col], waves[n1:, col]
        rows.append(
            jnp.concatenate([re * tc + im * ts, im * tc - re * ts], axis=1).astype(bf16)
        )
    waves = jnp.dot(jnp.concatenate(rows, axis=0), w2_ref[...], preferred_element_type=f32)
    mag = mag_ref[...]
    rows = []
    for fi in range(fold):
        low, high = edges_ref[0, step * fold + fi], edges_ref[1, step * fold + fi]
        passing = (mag >= low) & (mag <= high)
        block = waves[fi * n1 : (fi + 1) * n1]
        rows.append(
            jnp.concatenate(
                [
                    jnp.where(passing, block[:, :lanes], 0.0),
                    jnp.where(passing, block[:, lanes:], 0.0),
                ],
                axis=1,
            ).astype(bf16)
        )
    waves = jnp.dot(jnp.concatenate(rows, axis=0), v2_ref[...], preferred_element_type=f32)
    cols = []
    for fi in range(fold):
        block = waves[fi * n1 : (fi + 1) * n1] * scale_ref[0, step * fold + fi]
        re, im = block[:, :lanes], block[:, lanes:]
        cols.append(
            jnp.concatenate([re * tc - im * ts, im * tc + re * ts], axis=0).astype(bf16)
        )
    out = jnp.dot(v1_ref[...], jnp.concatenate(cols, axis=1), preferred_element_type=f32)
    for ri in range(2):
        for p in range(parts):
            r0 = (ri * parts + p) * devices
            piece = jnp.stack(
                [out[r0 : r0 + devices, fi * lanes : (fi + 1) * lanes] for fi in range(fold)]
            )
            o_ref[:, ri * fold : (ri + 1) * fold, p * lanes : (p + 1) * lanes] = jnp.swapaxes(
                piece, 0, 1
            ).astype(bf16)


def greet(me, devices):
    barrier = pltpu.get_barrier_semaphore()

    @pl.loop(1, devices)
    def _(off):
        pl.semaphore_signal(barrier, inc=1, device_id={"chan": lax.rem(me + off, devices)})

    pl.semaphore_wait(barrier, devices - 1)


def filter_kernel(fold, edges_ref, scale_ref, x_ref, *refs):
    tables, (out_ref, got_ref, mid_ref, sent, came) = refs[:6], refs[6:]
    devices, rows, _ = x_ref.shape
    chunks = rows // (2 * fold)
    me = lax.axis_index("chan")
    greet(me, devices)

    def piece(k):
        return pl.ds(pl.multiple_of(k * (2 * fold), 2 * fold), 2 * fold)

    def copy(way, k, peer, slot):
        src, dst = ((x_ref, got_ref), (mid_ref, out_ref))[way]
        return pltpu.make_async_remote_copy(
            src_ref=src.at[peer, piece(k)],
            dst_ref=dst.at[slot, piece(k)],
            send_sem=sent.at[way, k, peer],
            recv_sem=came.at[way, k, slot],
            device_id={"chan": peer},
        )

    def others(body):
        @pl.loop(1, devices)
        def _(off):
            body(lax.rem(me + off, devices))

    @pl.loop(0, chunks)
    def _(k):
        others(lambda peer: copy(0, k, peer, me).start())

    got_ref[me] = x_ref[me]

    @pl.loop(0, chunks)
    def _(k):
        others(lambda peer: copy(0, k, peer, peer).wait_recv())
        filter_chunk(
            fold, k, edges_ref, scale_ref, got_ref.at[:, piece(k), :], *tables, mid_ref.at[:, piece(k), :]
        )
        others(lambda peer: copy(1, k, peer, me).start())
        out_ref[me, piece(k), :] = mid_ref[me, piece(k), :]

    @pl.loop(0, chunks)
    def _(k):
        others(lambda peer: copy(0, k, peer, peer).wait_send())
        others(lambda peer: copy(1, k, peer, peer).wait())


def filter_exchange(spectrum, edges, scale, fold):
    devices, rows, channels = spectrum.shape
    tables = filter_tables(devices * channels, devices, channels // lanes)
    smem = pl.BlockSpec(memory_space=pltpu.SMEM)
    vmem = pl.BlockSpec(memory_space=pltpu.VMEM)
    sems = (2, rows // (2 * fold), devices)
    return pl.pallas_call(
        functools.partial(filter_kernel, fold),
        out_shape=jax.ShapeDtypeStruct(spectrum.shape, bf16),
        in_specs=[smem, smem] + [vmem] * (1 + len(tables)),
        out_specs=vmem,
        scratch_shapes=[
            pltpu.VMEM(spectrum.shape, bf16),
            pltpu.VMEM(spectrum.shape, bf16),
            pltpu.SemaphoreType.DMA(sems),
            pltpu.SemaphoreType.DMA(sems),
        ],
        compiler_params=pltpu.CompilerParams(
            vmem_limit_bytes=vmem_limit, collective_id=1, has_side_effects=True
        ),
        name="fan_filter",
    )(edges, scale, spectrum, *tables)


def filter_plain(gathered, edges, scale, fold):
    devices, rows, channels = gathered.shape
    full_count = devices * channels
    values = gathered.reshape(devices, rows // (2 * fold), 2, fold, channels)
    values = values.transpose(2, 1, 3, 0, 4).reshape(2, rows // 2, devices, channels)
    d, m = np.arange(devices), np.arange(channels)
    ad = 2.0 * np.pi * (d[:, None] * d[None, :] % devices) / devices
    am = 2.0 * np.pi * (m[:, None] * m[None, :] % channels) / channels
    at = 2.0 * np.pi * (d[:, None] * m[None, :]) / full_count
    wave = d[:, None] + devices * m[None, :]
    magnitude = jnp.asarray(np.minimum(wave, full_count - wave), jnp.int32)[None]

    def turn(layout, angle, pair, sign):
        c, s = jnp.asarray(np.cos(angle), f32), jnp.asarray(sign * np.sin(angle), f32)
        ein = functools.partial(jnp.einsum, layout, precision=highest)
        return ein(c, pair[0]) - ein(s, pair[1]), ein(c, pair[1]) + ein(s, pair[0])

    def twist(pair, sign):
        c, s = jnp.asarray(np.cos(at), f32), jnp.asarray(sign * np.sin(at), f32)
        return c * pair[0] - s * pair[1], c * pair[1] + s * pair[0]

    pair = (values[0].astype(f32), values[1].astype(f32))
    pair = twist(turn("kp,fpm->fkm", ad, pair, -1.0), -1.0)
    pair = turn("mn,fkm->fkn", am, pair, -1.0)
    passing = (magnitude >= edges[0][:, None, None]) & (magnitude <= edges[1][:, None, None])
    pair = tuple(jnp.where(passing, part, 0.0) for part in pair)
    pair = twist(turn("mn,fkn->fkm", am, pair, 1.0), 1.0)
    pair = turn("kp,fkm->fpm", ad, pair, 1.0)
    out = (jnp.stack(pair) * scale[0][None, :, None, None]).astype(bf16)
    out = out.reshape(2, rows // (2 * fold), fold, devices, channels).transpose(3, 1, 0, 2, 4)
    return out.reshape(devices, rows, channels)


def final_kernel(
    full_count, taps, readings, series_ref, extra_ref, det_ref, coef_ref, got_ref, more_ref, sent, came
):
    devices, rank, lag_count = series_ref.shape
    square = rank * rank
    span = extra_ref.shape[2] - square
    me = lax.axis_index("chan")
    greet(me, devices)

    def copies(peer, slot):
        pair = ((series_ref, got_ref), (extra_ref, more_ref))
        return [
            pltpu.make_async_remote_copy(
                src_ref=src.at[peer],
                dst_ref=dst.at[slot],
                send_sem=sent.at[n, peer],
                recv_sem=came.at[n, slot],
                device_id={"chan": peer},
            )
            for n, (src, dst) in enumerate(pair)
        ]

    @pl.loop(1, devices)
    def _(off):
        for copy in copies(lax.rem(me + off, devices), me):
            copy.start()

    got_ref[me] = series_ref[me]
    more_ref[me] = extra_ref[me]

    @pl.loop(1, devices)
    def _(off):
        peer = lax.rem(me + off, devices)
        for copy in copies(peer, peer):
            copy.wait()

    correlation = jnp.sum(got_ref[...].astype(f32), axis=0) * (2.0 / readings)
    extra = jnp.sum(more_ref[...], axis=0)
    window = extra[:, :span]
    packed = jnp.broadcast_to(extra[:, span:], (rank, square))
    spread = lax.broadcasted_iota(jnp.int32, packed.shape, 1)
    packed = jnp.where(
        spread // rank == lax.broadcasted_iota(jnp.int32, packed.shape, 0), packed, 0.0
    )
    pick = lax.broadcasted_iota(jnp.int32, (square, rank), 0) % rank
    pick = jnp.where(pick == lax.broadcasted_iota(jnp.int32, pick.shape, 1), 1.0, 0.0)
    gram = jnp.dot(packed, pick, precision=highest)
    row = lax.broadcasted_iota(jnp.int32, (window.shape[1], lag_count), 0)
    lag = row - lax.broadcasted_iota(jnp.int32, row.shape, 1)
    band = jnp.where((lag >= 0) & (lag < taps), 1.0, 0.0)
    energy = jnp.dot(
        jnp.broadcast_to(window, (8, window.shape[1])), band, precision=highest
    )[:1] * (2.0 / readings) ** 2
    level = energy / (full_count * taps) + 1e-06
    solved = correlation
    ids = lax.broadcasted_iota(jnp.int32, (rank, 1), 0)
    for k in range(rank):
        inverse = 1.0 / gram[k : k + 1, k : k + 1]
        pivot_g, pivot_c = gram[k : k + 1] * inverse, solved[k : k + 1] * inverse
        column = gram[:, k : k + 1]
        gram = jnp.where(ids == k, pivot_g, gram - column * pivot_g)
        solved = jnp.where(ids == k, pivot_c, solved - column * pivot_c)
    det_ref[...] = jnp.sum(correlation * solved, axis=0, keepdims=True) / (rank * level)
    coef_ref[...] = correlation / jnp.sqrt(level)


def local(waveforms, basis, bounds):
    devices = lax.axis_size("chan")
    position = lax.axis_index("chan")
    channels, readings = waveforms.shape
    rank, _, taps = basis.shape
    frequencies = bounds.shape[1]
    full_count = channels * devices
    bin_count = frequencies // devices
    fold = math.gcd(16, bin_count)
    lag_count = readings // devices

    table = jnp.asarray(time_table(frequencies, readings, fold), bf16)
    spectrum = time_spectrum(waveforms, table)
    flat = basis.reshape(rank, channels * taps)
    gram = jnp.einsum("ka,ja->kj", flat, flat, preferred_element_type=f32)
    turned = jnp.swapaxes(basis, 1, 2)

    order = bin_order(frequencies)[0].reshape(-1)
    edges = lax.dynamic_slice_in_dim(bounds[:, order], position * bin_count, bin_count, 1)
    scale = jnp.asarray(np.where(order == 0, 0.5, 1.0) / full_count, f32).reshape(1, -1)
    scale = lax.dynamic_slice_in_dim(scale, position * bin_count, bin_count, 1)
    spectrum = spectrum.reshape(devices, 2 * bin_count, channels)
    if channels % lanes == 0:
        filtered = filter_exchange(spectrum, edges, scale, fold)
    else:
        gathered = lax.all_to_all(spectrum, "chan", split_axis=0, concat_axis=0, tiled=True)
        passed = filter_plain(gathered, edges, scale, fold)
        filtered = lax.all_to_all(passed, "chan", split_axis=0, concat_axis=0, tiled=True)
    filtered = filtered.reshape(2 * frequencies, channels)

    power, series = power_and_series(turned, filtered, table, readings, fold)
    ahead = 1 + -(-taps // lag_count)
    span = -(-(lag_count + taps) // lanes) * lanes
    power = power.reshape(devices, lag_count)
    windows = jnp.concatenate([jnp.roll(power, -n, axis=0) for n in range(ahead)], axis=1)
    windows = jnp.pad(windows[:, : lag_count + taps], ((0, 0), (0, span - lag_count - taps)))
    gram = jnp.broadcast_to(gram.reshape(1, -1), (devices, rank * rank))
    extra = jnp.concatenate([windows, gram], axis=1)[:, None, :]
    series = series.astype(bf16).reshape(rank, devices, lag_count).transpose(1, 0, 2)
    vmem = pl.BlockSpec(memory_space=pltpu.VMEM)
    detection, coefficients = pl.pallas_call(
        functools.partial(final_kernel, full_count, taps, readings),
        out_shape=(
            jax.ShapeDtypeStruct((1, lag_count), f32),
            jax.ShapeDtypeStruct((rank, lag_count), f32),
        ),
        in_specs=[vmem, vmem],
        out_specs=(vmem, vmem),
        scratch_shapes=[
            pltpu.VMEM(series.shape, bf16),
            pltpu.VMEM(extra.shape, f32),
            pltpu.SemaphoreType.DMA((2, devices)),
            pltpu.SemaphoreType.DMA((2, devices)),
        ],
        compiler_params=pltpu.CompilerParams(
            vmem_limit_bytes=vmem_limit, collective_id=0, has_side_effects=True
        ),
        name="detect",
    )(series, extra)
    return (detection[0], coefficients)


def solution(mesh):
    in_specs = (P("chan", "groups"), P(None, "chan", None), P())
    out_specs = (P(("groups", "chan")), P(None, ("groups", "chan")))
    return jax.shard_map(local, mesh=mesh, in_specs=in_specs, out_specs=out_specs, check_vma=False)
```

```python
import functools
import math

import jax
import jax.numpy as jnp
import numpy as np
from jax import lax
from jax.experimental import pallas as pl
from jax.experimental.pallas import tpu as pltpu
from jax.sharding import PartitionSpec as P

radix = 12
half = radix // 2
lanes = 128
highest = lax.Precision.HIGHEST
bf16 = jnp.bfloat16
f32 = jnp.float32
vmem_limit = 60 * 1024 * 1024


def even_parts(x0, x6, s):
    r = math.sqrt(3.0) / 2.0
    s1, s2, s3, s4, s5 = s
    u, v = x0 + x6, x0 - x6
    e24, d24, e15, d15 = s2 + s4, s2 - s4, s1 + s5, s1 - s5
    even0, odd0 = u + e24, e15 + s3
    even1, odd1 = v + 0.5 * d24, r * d15
    even2, odd2 = u - 0.5 * e24, 0.5 * e15 - s3
    return (
        even0 + odd0,
        even1 + odd1,
        even2 + odd2,
        v - d24,
        even2 - odd2,
        even1 - odd1,
        even0 - odd0,
    )


def odd_parts(d):
    r = math.sqrt(3.0) / 2.0
    d1, d2, d3, d4, d5 = d
    e15, m15 = d1 + d5, d1 - d5
    odd1, even1 = 0.5 * e15 + d3, r * (d2 + d4)
    odd2, even2 = r * m15, r * (d2 - d4)
    return (odd1 + even1, odd2 + even2, e15 - d3, odd2 - even2, odd1 - even1)


def bin_order(frequencies):
    ids = np.arange(frequencies)
    groups = [np.concatenate([ids[ids % radix == 0], ids[ids % radix == half]])]
    signs = [np.ones(frequencies // half)]
    for q in range(1, half):
        plus, minus = ids[ids % radix == q], ids[ids % radix == radix - q]
        groups.append(np.concatenate([plus, minus]))
        signs.append(np.concatenate([np.ones(len(plus)), -np.ones(len(minus))]))
    return np.stack(groups), np.stack(signs)


def time_table(frequencies, readings, fold):
    width = readings // radix
    groups, signs = bin_order(frequencies)
    theta = (groups[:, :, None] * np.arange(width)[None, None, :] % readings) * (
        2.0 * np.pi / readings
    )
    cos, sin = np.cos(theta), np.sin(theta)
    sg = signs[:, :, None]
    real = np.concatenate([cos, -sg * sin], axis=2)
    imag = np.concatenate([-sin, -sg * cos], axis=2)
    first = (groups[0] % radix == 0)[:, None]
    real[0] = np.concatenate([np.where(first, cos[0], 0), np.where(first, 0, cos[0])], axis=1)
    imag[0] = np.concatenate([np.where(first, -sin[0], 0), np.where(first, 0, -sin[0])], axis=1)
    count = groups.shape[1]
    both = np.stack([real, imag], axis=1).reshape(half, 2, count // fold, fold, 2 * width)
    return both.transpose(0, 2, 1, 3, 4).reshape(half, 2 * count, 2 * width)


def row_bins(frequencies, fold):
    order = bin_order(frequencies)[0].reshape(-1, 1, fold)
    return np.broadcast_to(order, (order.shape[0], 2, fold)).reshape(-1)


def spectrum_kernel(blocks, x_ref, table_ref, out_ref, y_ref):
    rows, readings = x_ref.shape
    width = readings // radix
    step = pl.program_id(0)

    @pl.when(step < blocks)
    def _():
        @pl.loop(0, rows // 16)
        def _(r):
            rs = pl.ds(r * 16, 16)
            ys = pl.ds(step * rows + r * 16, 16)
            for b0 in range(0, width, lanes):
                x = [
                    x_ref[rs, a * width + b0 : a * width + b0 + lanes].astype(f32)
                    for a in range(radix)
                ]
                even = even_parts(x[0], x[half], [x[a] + x[radix - a] for a in range(1, half)])
                odd = odd_parts([x[a] - x[radix - a] for a in range(1, half)])
                left = slice(b0, b0 + lanes)
                right = slice(width + b0, width + b0 + lanes)
                y_ref[0, ys, left] = even[0].astype(bf16)
                y_ref[0, ys, right] = even[half].astype(bf16)
                for q in range(1, half):
                    y_ref[q, ys, left] = even[q].astype(bf16)
                    y_ref[q, ys, right] = odd[q - 1].astype(bf16)

    @pl.when(step >= blocks)
    def _():
        out_ref[...] = lax.dot_general(
            table_ref[0],
            y_ref[step - blocks],
            (((1,), (1,)), ((), ())),
            preferred_element_type=f32,
        ).astype(bf16)


def time_spectrum(waveforms, table):
    channels, readings = waveforms.shape
    block = lanes if channels % lanes == 0 else channels
    blocks = channels // block
    count = table.shape[1]
    group = lambda i: jnp.maximum(i - blocks, 0)
    return pl.pallas_call(
        functools.partial(spectrum_kernel, blocks),
        out_shape=jax.ShapeDtypeStruct((half * count, channels), bf16),
        grid=(blocks + half,),
        in_specs=[
            pl.BlockSpec((block, readings), lambda i: (jnp.minimum(i, blocks - 1), 0)),
            pl.BlockSpec((1,) + table.shape[1:], lambda i: (group(i), 0, 0)),
        ],
        out_specs=pl.BlockSpec((count, channels), lambda i: (group(i), 0)),
        scratch_shapes=[pltpu.VMEM((half, channels, 2 * readings // radix), bf16)],
        compiler_params=pltpu.CompilerParams(vmem_limit_bytes=vmem_limit),
        name="time_spectrum",
    )(waveforms, table)


def series_parts(zr, zs):
    even = even_parts(zr[0], zs[0], zr[1:])
    odd = odd_parts(zs[1:])
    series = [even[0]]
    series += [even[a] + odd[a - 1] for a in range(1, half)]
    series += [even[half]]
    series += [even[a] - odd[a - 1] for a in range(half - 1, 0, -1)]
    return series


def series_group(fold, group, block, b_ref, table, cos, sin, z_ref, c_ref):
    taps, count = cos.shape
    rank = c_ref.shape[1]
    z_ref[group] = lax.dot_general(
        block, table, (((0,), (0,)), ((), ())), preferred_element_type=f32
    )
    sums = lax.dot_general(
        b_ref[...], block, (((1,), (1,)), ((), ())), preferred_element_type=f32
    )
    first, second = [], []
    for r in range(rank):
        member = sums[r * taps : (r + 1) * taps]
        first.append(jnp.sum(member * cos, axis=0, keepdims=True))
        second.append(jnp.sum(member * sin, axis=0, keepdims=True))
    first = jnp.concatenate(first, axis=0)
    second = jnp.concatenate(second, axis=0)
    ids = lax.broadcasted_iota(jnp.int32, first.shape, 1)
    spectra = first + jnp.where(
        (ids // fold) % 2 == 0,
        -pltpu.roll(second, count - fold, 1),
        pltpu.roll(second, fold, 1),
    )
    high = spectra.astype(bf16)
    low = (spectra - high.astype(f32)).astype(bf16)
    c_ref[group] = jnp.dot(high, table, preferred_element_type=f32) + jnp.dot(
        low, table, preferred_element_type=f32
    )


def series_end(power_ref, out_ref, z_ref, c_ref):
    width = z_ref.shape[2] // 2
    power_ref[...] = jnp.zeros_like(power_ref)

    @pl.loop(0, z_ref.shape[1] // 16)
    def _(r):
        rs = pl.ds(r * 16, 16)
        for b0 in range(0, width, lanes):
            left = slice(b0, b0 + lanes)
            right = slice(width + b0, width + b0 + lanes)
            parts = series_parts(
                [z_ref[g, rs, left] for g in range(half)],
                [z_ref[g, rs, right] for g in range(half)],
            )
            for a, value in enumerate(parts):
                square = value * value
                power_ref[a, :, left] += square[:8] + square[8:]

    parts = series_parts(
        [c_ref[g, :, :width] for g in range(half)],
        [c_ref[g, :, width:] for g in range(half)],
    )
    for a, value in enumerate(parts):
        out_ref[:, a * width : (a + 1) * width] = value


def series_kernel(fold, b_ref, f_ref, t_ref, cos_ref, sin_ref, power_ref, out_ref, z_ref, c_ref):
    group = pl.program_id(0)
    series_group(
        fold, group, f_ref[...], b_ref, t_ref[0], cos_ref[...], sin_ref[...], z_ref, c_ref
    )

    @pl.when(group == half - 1)
    def _():
        series_end(power_ref, out_ref, z_ref, c_ref)


def power_and_series(turned, filtered, table, readings, fold):
    rank, taps, channels = turned.shape
    rows = filtered.shape[0]
    count, width = table.shape[1], table.shape[2] // 2
    bins = row_bins(rows // 2, fold)
    angle = 2.0 * np.pi * (np.arange(taps)[:, None] * bins[None, :] % readings) / readings
    power, series = pl.pallas_call(
        functools.partial(series_kernel, fold),
        out_shape=(
            jax.ShapeDtypeStruct((radix, 8, width), f32),
            jax.ShapeDtypeStruct((rank, readings), f32),
        ),
        grid=(half,),
        in_specs=[
            pl.BlockSpec((rank * taps, channels), lambda i: (0, 0)),
            pl.BlockSpec((count, channels), lambda i: (i, 0)),
            pl.BlockSpec((1,) + table.shape[1:], lambda i: (i, 0, 0)),
            pl.BlockSpec((taps, count), lambda i: (0, i)),
            pl.BlockSpec((taps, count), lambda i: (0, i)),
        ],
        out_specs=(
            pl.BlockSpec((radix, 8, width), lambda i: (0, 0, 0)),
            pl.BlockSpec((rank, readings), lambda i: (0, 0)),
        ),
        scratch_shapes=[
            pltpu.VMEM((half, channels, 2 * width), f32),
            pltpu.VMEM((half, rank, 2 * width), f32),
        ],
        compiler_params=pltpu.CompilerParams(vmem_limit_bytes=vmem_limit),
        name="power_and_series",
    )(
        turned.reshape(rank * taps, channels),
        filtered,
        table,
        jnp.asarray(np.cos(angle), f32),
        jnp.asarray(np.sin(angle), f32),
    )
    return jnp.sum(power, axis=1).reshape(-1), series


def filter_tables(full_count, block_count, parts):
    n2 = lanes
    n1 = full_count // n2
    order = np.arange(n1).reshape(block_count, parts).T.reshape(-1)
    k1, k2, j = np.arange(n1), np.arange(n2), np.arange(n2)
    a1 = 2.0 * np.pi * ((k1[:, None] * order[None, :]) % n1) / n1
    a2 = 2.0 * np.pi * ((j[:, None] * k2[None, :]) % n2) / n2
    at = 2.0 * np.pi * ((k1[:, None] * j[None, :]) % full_count) / full_count
    c1, s1, c2, s2 = np.cos(a1), np.sin(a1), np.cos(a2), np.sin(a2)
    first = np.block([[c1, s1], [-s1, c1]])
    second = np.block([[c2, -s2], [s2, c2]])
    twist = np.stack([np.cos(at), np.sin(at)])
    wave = k1[:, None] + n1 * k2[None, :]
    magnitude = np.minimum(wave, full_count - wave).astype(np.int32)
    return (
        jnp.asarray(first, bf16),
        jnp.asarray(second, bf16),
        jnp.asarray(first.T.copy(), bf16),
        jnp.asarray(second.T.copy(), bf16),
        jnp.asarray(twist, f32),
        jnp.asarray(magnitude),
    )


def filter_chunk(fold, step, edges_ref, scale_ref, x_ref, w1_ref, w2_ref, v1_ref, v2_ref, tw_ref, mag_ref, o_ref):
    devices = x_ref.shape[0]
    parts = x_ref.shape[2] // lanes
    n1 = mag_ref.shape[0]
    pieces = []
    for ri in range(2):
        for p in range(parts):
            piece = x_ref[:, ri * fold : (ri + 1) * fold, p * lanes : (p + 1) * lanes]
            pieces.append(jnp.swapaxes(piece.astype(f32), 0, 1).astype(bf16))
    stacked = jnp.concatenate(
        [jnp.concatenate([piece[fi] for piece in pieces], axis=0) for fi in range(fold)], axis=1
    )
    waves = jnp.dot(w1_ref[...], stacked, preferred_element_type=f32)
    tc, ts = tw_ref[0], tw_ref[1]
    rows = []
    for fi in range(fold):
        col = slice(fi * lanes, (fi + 1) * lanes)
        re, im = waves[:n1, col], waves[n1:, col]
        rows.append(
            jnp.concatenate([re * tc + im * ts, im * tc - re * ts], axis=1).astype(bf16)
        )
    waves = jnp.dot(jnp.concatenate(rows, axis=0), w2_ref[...], preferred_element_type=f32)
    mag = mag_ref[...]
    rows = []
    for fi in range(fold):
        low, high = edges_ref[0, step * fold + fi], edges_ref[1, step * fold + fi]
        passing = (mag >= low) & (mag <= high)
        block = waves[fi * n1 : (fi + 1) * n1]
        rows.append(
            jnp.concatenate(
                [
                    jnp.where(passing, block[:, :lanes], 0.0),
                    jnp.where(passing, block[:, lanes:], 0.0),
                ],
                axis=1,
            ).astype(bf16)
        )
    waves = jnp.dot(jnp.concatenate(rows, axis=0), v2_ref[...], preferred_element_type=f32)
    cols = []
    for fi in range(fold):
        block = waves[fi * n1 : (fi + 1) * n1] * scale_ref[0, step * fold + fi]
        re, im = block[:, :lanes], block[:, lanes:]
        cols.append(
            jnp.concatenate([re * tc - im * ts, im * tc + re * ts], axis=0).astype(bf16)
        )
    out = jnp.dot(v1_ref[...], jnp.concatenate(cols, axis=1), preferred_element_type=f32)
    for ri in range(2):
        for p in range(parts):
            r0 = (ri * parts + p) * devices
            piece = jnp.stack(
                [out[r0 : r0 + devices, fi * lanes : (fi + 1) * lanes] for fi in range(fold)]
            )
            o_ref[:, ri * fold : (ri + 1) * fold, p * lanes : (p + 1) * lanes] = jnp.swapaxes(
                piece, 0, 1
            ).astype(bf16)


def greet(me, devices):
    barrier = pltpu.get_barrier_semaphore()

    @pl.loop(1, devices)
    def _(off):
        pl.semaphore_signal(barrier, inc=1, device_id={"chan": lax.rem(me + off, devices)})

    pl.semaphore_wait(barrier, devices - 1)


def filter_kernel(fold, edges_ref, scale_ref, x_ref, *refs):
    tables, refs = refs[:6], refs[6:]
    b_ref, t_ref, cos_ref, sin_ref, power_ref, series_ref, *refs = refs
    got_ref, mid_ref, out_ref, z_ref, c_ref, sent, came = refs
    chunks, devices, rows, channels = x_ref.shape
    per_chunk = half // chunks
    count = t_ref.shape[1]
    me = lax.axis_index("chan")
    greet(me, devices)

    def copy(way, k, peer, slot):
        src, dst = ((x_ref, got_ref), (mid_ref, out_ref))[way]
        return pltpu.make_async_remote_copy(
            src_ref=src.at[k, peer],
            dst_ref=dst.at[k, slot],
            send_sem=sent.at[way, k, peer],
            recv_sem=came.at[way, k, slot],
            device_id={"chan": peer},
        )

    def others(body):
        @pl.loop(1, devices)
        def _(off):
            body(lax.rem(me + off, devices))

    @pl.loop(0, chunks)
    def _(k):
        others(lambda peer: copy(0, k, peer, me).start())
        got_ref[k, me] = x_ref[k, me]

    @pl.loop(0, chunks)
    def _(k):
        others(lambda peer: copy(0, k, peer, peer).wait_recv())
        filter_chunk(
            fold, k, edges_ref, scale_ref, got_ref.at[k], *tables, mid_ref.at[k]
        )
        others(lambda peer: copy(1, k, peer, me).start())
        out_ref[k, me] = mid_ref[k, me]

    @pl.loop(0, chunks)
    def _(k):
        others(lambda peer: copy(1, k, peer, peer).wait_recv())
        for n in range(per_chunk):
            part = devices // per_chunk
            block = out_ref[k, n * part : (n + 1) * part].reshape(count, channels)
            group = k * per_chunk + n
            series_group(
                fold, group, block, b_ref, t_ref[group], cos_ref[group], sin_ref[group], z_ref, c_ref
            )

    series_end(power_ref, series_ref, z_ref, c_ref)

    @pl.loop(0, chunks)
    def _(k):
        others(lambda peer: copy(0, k, peer, peer).wait_send())
        others(lambda peer: copy(1, k, peer, peer).wait_send())


def filter_exchange(spectrum, edges, scale, turned, table, readings, fold):
    chunks, devices, rows, channels = spectrum.shape
    rank, taps, _ = turned.shape
    count, width = table.shape[1], table.shape[2] // 2
    bins = row_bins(chunks * devices * fold, fold)
    angle = 2.0 * np.pi * (np.arange(taps)[:, None] * bins[None, :] % readings) / readings
    angle = angle.reshape(taps, half, count).transpose(1, 0, 2)
    tables = filter_tables(devices * channels, devices, channels // lanes)
    smem = pl.BlockSpec(memory_space=pltpu.SMEM)
    vmem = pl.BlockSpec(memory_space=pltpu.VMEM)
    sems = (2, chunks, devices)
    power, series = pl.pallas_call(
        functools.partial(filter_kernel, fold),
        out_shape=(
            jax.ShapeDtypeStruct((radix, 8, width), f32),
            jax.ShapeDtypeStruct((rank, readings), f32),
        ),
        in_specs=[smem, smem] + [vmem] * (5 + len(tables)),
        out_specs=(vmem, vmem),
        scratch_shapes=[
            pltpu.VMEM(spectrum.shape, bf16),
            pltpu.VMEM(spectrum.shape, bf16),
            pltpu.VMEM(spectrum.shape, bf16),
            pltpu.VMEM((half, channels, 2 * width), f32),
            pltpu.VMEM((half, rank, 2 * width), f32),
            pltpu.SemaphoreType.DMA(sems),
            pltpu.SemaphoreType.DMA(sems),
        ],
        compiler_params=pltpu.CompilerParams(
            vmem_limit_bytes=vmem_limit, collective_id=1, has_side_effects=True
        ),
        name="fan_filter",
    )(
        edges,
        scale,
        spectrum,
        *tables,
        turned.reshape(rank * taps, channels),
        table,
        jnp.asarray(np.cos(angle), f32),
        jnp.asarray(np.sin(angle), f32),
    )
    return jnp.sum(power, axis=1).reshape(-1), series


def filter_plain(gathered, edges, scale, fold):
    devices, rows, channels = gathered.shape
    full_count = devices * channels
    values = gathered.reshape(devices, rows // (2 * fold), 2, fold, channels)
    values = values.transpose(2, 1, 3, 0, 4).reshape(2, rows // 2, devices, channels)
    d, m = np.arange(devices), np.arange(channels)
    ad = 2.0 * np.pi * (d[:, None] * d[None, :] % devices) / devices
    am = 2.0 * np.pi * (m[:, None] * m[None, :] % channels) / channels
    at = 2.0 * np.pi * (d[:, None] * m[None, :]) / full_count
    wave = d[:, None] + devices * m[None, :]
    magnitude = jnp.asarray(np.minimum(wave, full_count - wave), jnp.int32)[None]

    def turn(layout, angle, pair, sign):
        c, s = jnp.asarray(np.cos(angle), f32), jnp.asarray(sign * np.sin(angle), f32)
        ein = functools.partial(jnp.einsum, layout, precision=highest)
        return ein(c, pair[0]) - ein(s, pair[1]), ein(c, pair[1]) + ein(s, pair[0])

    def twist(pair, sign):
        c, s = jnp.asarray(np.cos(at), f32), jnp.asarray(sign * np.sin(at), f32)
        return c * pair[0] - s * pair[1], c * pair[1] + s * pair[0]

    pair = (values[0].astype(f32), values[1].astype(f32))
    pair = twist(turn("kp,fpm->fkm", ad, pair, -1.0), -1.0)
    pair = turn("mn,fkm->fkn", am, pair, -1.0)
    passing = (magnitude >= edges[0][:, None, None]) & (magnitude <= edges[1][:, None, None])
    pair = tuple(jnp.where(passing, part, 0.0) for part in pair)
    pair = twist(turn("mn,fkn->fkm", am, pair, 1.0), 1.0)
    pair = turn("kp,fkm->fpm", ad, pair, 1.0)
    out = (jnp.stack(pair) * scale[0][None, :, None, None]).astype(bf16)
    out = out.reshape(2, rows // (2 * fold), fold, devices, channels).transpose(3, 1, 0, 2, 4)
    return out.reshape(devices, rows, channels)


def final_kernel(
    full_count, taps, readings, series_ref, extra_ref, det_ref, coef_ref, got_ref, more_ref, sent, came
):
    devices, rank, lag_count = series_ref.shape
    square = rank * rank
    span = extra_ref.shape[2] - square
    me = lax.axis_index("chan")
    greet(me, devices)

    def copies(peer, slot):
        pair = ((series_ref, got_ref), (extra_ref, more_ref))
        return [
            pltpu.make_async_remote_copy(
                src_ref=src.at[peer],
                dst_ref=dst.at[slot],
                send_sem=sent.at[n, peer],
                recv_sem=came.at[n, slot],
                device_id={"chan": peer},
            )
            for n, (src, dst) in enumerate(pair)
        ]

    @pl.loop(1, devices)
    def _(off):
        for copy in copies(lax.rem(me + off, devices), me):
            copy.start()

    got_ref[me] = series_ref[me]
    more_ref[me] = extra_ref[me]

    @pl.loop(1, devices)
    def _(off):
        peer = lax.rem(me + off, devices)
        for copy in copies(peer, peer):
            copy.wait()

    correlation = jnp.sum(got_ref[...].astype(f32), axis=0) * (2.0 / readings)
    extra = jnp.sum(more_ref[...], axis=0)
    window = extra[:, :span]
    packed = jnp.broadcast_to(extra[:, span:], (rank, square))
    spread = lax.broadcasted_iota(jnp.int32, packed.shape, 1)
    packed = jnp.where(
        spread // rank == lax.broadcasted_iota(jnp.int32, packed.shape, 0), packed, 0.0
    )
    pick = lax.broadcasted_iota(jnp.int32, (square, rank), 0) % rank
    pick = jnp.where(pick == lax.broadcasted_iota(jnp.int32, pick.shape, 1), 1.0, 0.0)
    gram = jnp.dot(packed, pick, precision=highest)
    row = lax.broadcasted_iota(jnp.int32, (window.shape[1], lag_count), 0)
    lag = row - lax.broadcasted_iota(jnp.int32, row.shape, 1)
    band = jnp.where((lag >= 0) & (lag < taps), 1.0, 0.0)
    energy = jnp.dot(
        jnp.broadcast_to(window, (8, window.shape[1])), band, precision=highest
    )[:1] * (2.0 / readings) ** 2
    level = energy / (full_count * taps) + 1e-06
    solved = correlation
    ids = lax.broadcasted_iota(jnp.int32, (rank, 1), 0)
    for k in range(rank):
        inverse = 1.0 / gram[k : k + 1, k : k + 1]
        pivot_g, pivot_c = gram[k : k + 1] * inverse, solved[k : k + 1] * inverse
        column = gram[:, k : k + 1]
        gram = jnp.where(ids == k, pivot_g, gram - column * pivot_g)
        solved = jnp.where(ids == k, pivot_c, solved - column * pivot_c)
    det_ref[...] = jnp.sum(correlation * solved, axis=0, keepdims=True) / (rank * level)
    coef_ref[...] = correlation / jnp.sqrt(level)


def local(waveforms, basis, bounds):
    devices = lax.axis_size("chan")
    position = lax.axis_index("chan")
    channels, readings = waveforms.shape
    rank, _, taps = basis.shape
    frequencies = bounds.shape[1]
    full_count = channels * devices
    bin_count = frequencies // devices
    fold = math.gcd(16, bin_count)
    lag_count = readings // devices

    table = jnp.asarray(time_table(frequencies, readings, fold), bf16)
    spectrum = time_spectrum(waveforms, table)
    flat = basis.reshape(rank, channels * taps)
    gram = jnp.einsum("ka,ja->kj", flat, flat, preferred_element_type=f32)
    turned = jnp.swapaxes(basis, 1, 2)

    order = bin_order(frequencies)[0].reshape(-1)
    chunks = bin_count // fold
    fused = channels % lanes == 0 and half % chunks == 0 and devices % (half // chunks) == 0
    if fused:
        order = order.reshape(chunks, devices, fold).transpose(1, 0, 2).reshape(-1)
    edges = lax.dynamic_slice_in_dim(bounds[:, order], position * bin_count, bin_count, 1)
    scale = jnp.asarray(np.where(order == 0, 0.5, 1.0) / full_count, f32).reshape(1, -1)
    scale = lax.dynamic_slice_in_dim(scale, position * bin_count, bin_count, 1)
    if fused:
        spectrum = spectrum.reshape(chunks, devices, 2 * fold, channels)
        power, series = filter_exchange(spectrum, edges, scale, turned, table, readings, fold)
    else:
        spectrum = spectrum.reshape(devices, 2 * bin_count, channels)
        gathered = lax.all_to_all(spectrum, "chan", split_axis=0, concat_axis=0, tiled=True)
        passed = filter_plain(gathered, edges, scale, fold)
        filtered = lax.all_to_all(passed, "chan", split_axis=0, concat_axis=0, tiled=True)
        filtered = filtered.reshape(2 * frequencies, channels)
        power, series = power_and_series(turned, filtered, table, readings, fold)
    ahead = 1 + -(-taps // lag_count)
    span = -(-(lag_count + taps) // lanes) * lanes
    power = power.reshape(devices, lag_count)
    windows = jnp.concatenate([jnp.roll(power, -n, axis=0) for n in range(ahead)], axis=1)
    windows = jnp.pad(windows[:, : lag_count + taps], ((0, 0), (0, span - lag_count - taps)))
    gram = jnp.broadcast_to(gram.reshape(1, -1), (devices, rank * rank))
    extra = jnp.concatenate([windows, gram], axis=1)[:, None, :]
    series = series.astype(bf16).reshape(rank, devices, lag_count).transpose(1, 0, 2)
    vmem = pl.BlockSpec(memory_space=pltpu.VMEM)
    detection, coefficients = pl.pallas_call(
        functools.partial(final_kernel, full_count, taps, readings),
        out_shape=(
            jax.ShapeDtypeStruct((1, lag_count), f32),
            jax.ShapeDtypeStruct((rank, lag_count), f32),
        ),
        in_specs=[vmem, vmem],
        out_specs=(vmem, vmem),
        scratch_shapes=[
            pltpu.VMEM(series.shape, bf16),
            pltpu.VMEM(extra.shape, f32),
            pltpu.SemaphoreType.DMA((2, devices)),
            pltpu.SemaphoreType.DMA((2, devices)),
        ],
        compiler_params=pltpu.CompilerParams(
            vmem_limit_bytes=vmem_limit, collective_id=0, has_side_effects=True
        ),
        name="detect",
    )(series, extra)
    return (detection[0], coefficients)


def solution(mesh):
    in_specs = (P("chan", "groups"), P(None, "chan", None), P())
    out_specs = (P(("groups", "chan")), P(None, ("groups", "chan")))
    return jax.shard_map(local, mesh=mesh, in_specs=in_specs, out_specs=out_specs, check_vma=False)
```
